1024 devices in a mesh: ctx: 16 (over x, y), ch: 64 (over z, core).
Axes of the slice: x: 4, y: 4, z: 32, core: 2. Of those that a mesh axis runs over, the one named last changes fastest.
Arguments:
- proj: bfloat16 [3, 4096, 4096], P(None, 'ch', 'ctx'), may hold values from -4 to 4
- scale_exp: int32 [3, 4096, 32], P(None, 'ch', 'ctx'), may hold values from -1 to 1
- filt: bfloat16 [4096, 4096], P('ch'), may hold values from -8 to 8
- reach: int32 [4096], P('ch'), may hold values from 0 to 4
- skip: float32 [4096], P('ch'), may hold values from 0.1 to 1.9
- cotangent: bfloat16 [4096, 4096], P('ch', 'ctx'), may hold values from -6 to 6
Outputs:
- scaled_out: bfloat16 [4096, 4096], P('ch', 'ctx')
- token_max: float32 [4096], P('ctx')
- gradients: bfloat16 [3, 4096, 4096], P(None, 'ch', 'ctx')
- filter_grad: float32 [4096, 4096], P('ch', 'ctx')
The draws below stay inside these ranges and needn't reach their ends.
All inputs are finite; a program needn't handle non-finite values. Where the reference program divides by a largest or mean magnitude, that divisor is 1e-20 or more.
Results may differ from the reference program's by a relative error of at most 0.015.
Values may be sent and summed in bfloat16 or wider, within the bound.
A program may use at most 32 MiB of HBM per device.

```python
import math
import jax
import jax.numpy as jnp
from jax import lax

D = 4096
BLOCK = 128
SEQ = 4096


def draw_reach(key, part):
    raw_class = jax.random.randint(key, (D,), 0, 7, dtype=jnp.int32)
    return jnp.minimum(raw_class, 4)


def set_ends(entries, key, low, largest):
    shape = entries.shape
    index_at = [jax.random.randint(jax.random.fold_in(key, axis), (), 0, shape[axis]) for axis in range(len(shape))]
    entries = entries.at[tuple(index_at)].set(low)
    longest = shape.index(max(shape))
    index_at[longest] = (index_at[longest] + 1) % shape[longest]
    return entries.at[tuple(index_at)].set(largest)


def level_of(key, shape, shards, low, largest):
    loudness = 1.0
    for position, parts in shards:
        steps = jax.random.uniform(jax.random.fold_in(jax.random.fold_in(key, 6), position), (parts,), jnp.float32, low / len(shards), largest / len(shards))
        loudness = loudness * jnp.repeat(jnp.exp(steps), shape[position] // parts).reshape((-1,) + (1,) * (len(shape) - 1 - position))
    return loudness


def normal_values(own_key, shape, deviation, most, cuts=(), kind=jnp.bfloat16):
    values = jax.random.normal(own_key, shape, jnp.float32) * deviation
    if len(cuts) > 0:
        values = level_of(own_key, shape, cuts, -0.22, 0.18) * values
    return jnp.clip(values, min=-most, max=most).astype(kind)


def setup_inputs(seed: int = 0) -> dict:
    arg_keys = jax.random.split(jax.random.key(seed), 7)
    return {
        "proj": normal_values(arg_keys[0], (3, D, SEQ), 1.0, 4.0, ((1, 64), (2, 16))),
        "scale_exp": set_ends(jax.random.randint(arg_keys[1], (3, D, SEQ // BLOCK), -1, 2), jax.random.fold_in(arg_keys[1], 1), -1, 1).astype(jnp.int32),
        "filt": normal_values(arg_keys[2], (D, SEQ), 2.0, 8.0, ((0, 64),)),
        "reach": draw_reach(jax.random.fold_in(arg_keys[6], 71), 0),
        "skip": jnp.clip(1.0 + 0.18 * jax.random.normal(arg_keys[4], (D,), jnp.float32), 0.1, 1.9),
        "cotangent": normal_values(arg_keys[5], (D, SEQ), 1.0, 6.0, ((0, 64), (1, 16))),
    }


REACH_DIVISORS = (64, 32, 16, 4, 1)

def reference(proj, scale_exp, filt, reach, skip, cotangent):
    groups, channels, length = proj.shape
    scaled = jnp.exp2(scale_exp.astype(jnp.float32))
    dequant = (proj.astype(jnp.float32).reshape(groups, channels, length // BLOCK, BLOCK) * scaled[..., None]).reshape(groups, channels, length)
    queries = dequant[0]
    keys_deq = dequant[1]
    values_deq = dequant[2]
    mixed_bf = (keys_deq * values_deq).astype(jnp.bfloat16)
    mixed_f = lax.optimization_barrier(mixed_bf).astype(jnp.float32)
    divisors = jnp.array(REACH_DIVISORS, dtype=jnp.int32)
    reach_len = (SEQ // jnp.take(divisors, reach)).astype(jnp.int32)
    tap_index = jnp.arange(SEQ, dtype=jnp.int32)
    in_reach = (tap_index[None, :] < reach_len[:, None]).astype(jnp.float32)
    fscale = 1.0 / math.sqrt(SEQ)
    kernel = filt.astype(jnp.float32) * fscale * in_reach
    doubled = 2 * SEQ
    mixed_spec = jnp.fft.rfft(mixed_f, n=doubled, axis=1)
    kernel_spec = jnp.fft.rfft(kernel, n=doubled, axis=1)
    conv_out = jnp.fft.irfft(mixed_spec * kernel_spec, n=doubled, axis=1)[:, :SEQ] + skip[:, None] * mixed_f
    response = queries * conv_out
    token_max = lax.optimization_barrier(jnp.max(jnp.abs(response), axis=0))
    scaled_out = (response / (token_max + 1e-06)[None, :]).astype(jnp.bfloat16)
    upstream = cotangent.astype(jnp.float32)
    pulled_bf = (upstream * queries).astype(jnp.bfloat16)
    pulled = lax.optimization_barrier(pulled_bf).astype(jnp.float32)
    pulled_spec = jnp.fft.rfft(pulled, n=doubled, axis=1)
    grad_mixed = jnp.fft.irfft(jnp.conj(kernel_spec) * pulled_spec, n=doubled, axis=1)[:, :SEQ] + skip[:, None] * pulled
    gradients = jnp.stack([upstream * conv_out, grad_mixed * values_deq, grad_mixed * keys_deq]).astype(jnp.bfloat16)
    filter_grad = jnp.fft.irfft(jnp.conj(mixed_spec) * pulled_spec, n=doubled, axis=1)[:, :SEQ] * fscale * in_reach
    return (scaled_out, token_max, gradients, filter_grad)
```

```python
import functools
import math

import jax
import jax.numpy as jnp
from jax import lax
from jax.experimental import pallas as pl
from jax.experimental.pallas import tpu as pltpu
from jax.sharding import PartitionSpec as P

REACH_DIVISORS = (64, 32, 16, 4, 1)
MESH = pl.DeviceIdType.MESH
LANES = 128
CORES = 2
NT = (((1,), (1,)), ((), ()))


def z_windows(chips):
    if chips == 32:
        return tuple(range(-5, 6)), (0, -11, 11)
    return tuple(range(chips)), (0,)


def fine_shifts(row, dst):
    width = row.shape[1]
    strip = pltpu.roll(jnp.broadcast_to(row, (8, width)), 0, 1, stride=1, stride_axis=0)
    lane = lax.broadcasted_iota(jnp.int32, (16, LANES), 1)
    sub = lax.broadcasted_iota(jnp.int32, (16, LANES), 0)
    for k in range(LANES // 16):
        low = strip if k == 0 else pltpu.roll(strip, 16 * k, 1)
        both = jnp.concatenate([low, pltpu.roll(strip, 16 * k + 8, 1)], axis=0)
        first = jnp.where(lane >= sub + 16 * k, both[:, :LANES], 0.0)
        dst[16 * k : 16 * k + 16, :LANES] = first.astype(jnp.bfloat16)
        dst[16 * k : 16 * k + 16, LANES:] = both[:, LANES:].astype(jnp.bfloat16)


def kernel(
    parts, chips, chans, seq,
    aux, proj, cot, filt,
    so_ref, tm_ref, gr_ref, fg_ref,
    send_m, send_p, send_y, send_g, send_f,
    recv_m, recv_p, recv_y, recv_g, recv_f,
    taps_bf, taps, fine, pads, left, rev,
    lm, win1, wsend, win2,
    taps_sem, ctx_send, ctx_recv, s1_send, s1_recv, s2_send, s2_recv,
):
    own = chans // parts
    rows = 2 * own
    fscale = 1.0 / math.sqrt(seq)
    me = lax.axis_index("ctx")
    ch = lax.axis_index("ch")
    zpos = ch // CORES
    core = ch % CORES
    off1, off2 = z_windows(chips)
    n1, n2 = len(off1), len(off2)
    self1 = off1.index(0)

    def peer_of(step):
        return lax.rem(me + step, parts)

    def chip_dev(offset, side):
        return {"ch": lax.rem(zpos + (offset + chips), chips) * CORES + side}

    per_tile = 16 // own
    tile = pl.multiple_of(me // per_tile * 16, 16)
    tap_copy = pltpu.make_async_copy(filt.at[pl.ds(tile, 16), :], taps_bf, taps_sem)
    tap_copy.start()

    barrier = pltpu.get_barrier_semaphore()

    def greet(step, carry):
        pl.semaphore_signal(barrier, inc=1, device_id={"ctx": peer_of(step)}, device_id_type=MESH)
        return carry

    lax.fori_loop(1, parts, greet, 0)
    greeted = parts - 1
    for offset in off1 + off2[1:]:
        if offset == 0:
            pl.semaphore_signal(barrier, inc=1, device_id=chip_dev(0, 1 - core), device_id_type=MESH)
            greeted += 1
        else:
            for side in range(CORES):
                pl.semaphore_signal(barrier, inc=1, device_id=chip_dev(offset, side), device_id_type=MESH)
                greeted += 1

    def column(index):
        return aux[:, index : index + 1]

    def dequant(group, half):
        values = proj[group, :, LANES * half : LANES * (half + 1)].astype(jnp.float32)
        return values * column(2 * group + half)

    def upstream(half):
        return cot[:, LANES * half : LANES * (half + 1)].astype(jnp.float32)

    def mixed_of(half):
        return (dequant(1, half) * dequant(2, half)).astype(jnp.bfloat16).astype(jnp.float32)

    def pulled_of(half):
        return (upstream(half) * dequant(0, half)).astype(jnp.bfloat16).astype(jnp.float32)

    for half in range(2):
        send_m[pl.ds(half, chans, stride=2), :] = mixed_of(half)
        send_p[pl.ds(half, chans, stride=2), :] = pulled_of(half)

    mine = pl.ds(pl.multiple_of(rows * me, rows), rows)

    def exchange(which, src, dst):
        def copy(step):
            peer = peer_of(step)
            return pltpu.make_async_remote_copy(
                src_ref=src.at[pl.ds(pl.multiple_of(rows * peer, rows), rows), :],
                dst_ref=dst.at[mine, :],
                send_sem=ctx_send.at[which, peer],
                recv_sem=ctx_recv.at[which, me],
                device_id={"ctx": peer},
                device_id_type=MESH,
            )

        def arrival(step):
            peer = peer_of(step)
            return pltpu.make_async_remote_copy(
                src_ref=src.at[mine, :],
                dst_ref=dst.at[pl.ds(pl.multiple_of(rows * peer, rows), rows), :],
                send_sem=ctx_send.at[which, me],
                recv_sem=ctx_recv.at[which, peer],
                device_id={"ctx": peer},
                device_id_type=MESH,
            )

        def start():
            def go(step, carry):
                copy(step).start()
                return carry

            lax.fori_loop(1, parts, go, 0)
            dst[mine, :] = src[mine, :]

        def wait_recv():
            def go(step, carry):
                arrival(step).wait_recv()
                return carry

            lax.fori_loop(1, parts, go, 0)

        def wait_send():
            def go(step, carry):
                copy(step).wait_send()
                return carry

            lax.fori_loop(1, parts, go, 0)

        return start, wait_recv, wait_send

    m_start, m_recv, m_sent = exchange(0, send_m, recv_m)
    p_start, p_recv, p_sent = exchange(1, send_p, recv_p)
    y_start, y_recv, y_sent = exchange(2, send_y, recv_y)
    g_start, g_recv, g_sent = exchange(3, send_g, recv_g)
    f_start, f_recv, f_sent = exchange(4, send_f, recv_f)

    pl.semaphore_wait(barrier, greeted)
    m_start()
    p_start()

    tap_copy.wait()
    taps[...] = taps_bf[...].astype(jnp.float32)
    lag = lax.broadcasted_iota(jnp.int32, (1, seq), 1).astype(jnp.float32)
    for j in range(own):
        row = taps[pl.ds(me % per_tile * own + j, 1), :]
        reach = aux[pl.ds(me * own + j, 1), :][:, 7:8]
        fine_shifts(jnp.where(lag < reach, row, 0.0), fine.at[j, 0:LANES])

    flip = (
        lax.broadcasted_iota(jnp.int32, (LANES, LANES), 0)
        + lax.broadcasted_iota(jnp.int32, (LANES, LANES), 1)
        == LANES - 1
    ).astype(jnp.float32).astype(jnp.bfloat16)

    def reverse(values):
        return jnp.dot(values, flip, preferred_element_type=jnp.float32)

    m_recv()
    rev[...] = reverse(recv_m[...].astype(jnp.bfloat16))
    zeros = jnp.zeros((parts, LANES), jnp.float32)
    for slot in range(2):
        pads[slot, 0:parts, :] = zeros
    for j in range(own):
        pads[0, parts : 2 * parts, :] = rev[pl.ds(2 * j + 1, parts, stride=rows), :]
        pads[1, parts : 2 * parts, :] = rev[pl.ds(2 * j, parts, stride=rows), :]
        for n in range(2 * parts + 1):
            at = parts - n // 2
            block = pads[n % 2, at : at + parts, :].astype(jnp.bfloat16)
            if n < 2 * parts:
                left[0:parts, LANES * n : LANES * (n + 1)] = block
            if n >= 1:
                left[parts : 2 * parts, LANES * (n - 1) : LANES * n] = block
        out = lax.dot_general(left[...], fine[j, 0:LANES, :], NT, preferred_element_type=jnp.float32)
        top = out.astype(jnp.bfloat16)
        rest = (out - top.astype(jnp.float32)).astype(jnp.bfloat16)
        back = reverse(top) + reverse(rest)
        send_y[pl.ds(2 * j, parts, stride=rows), :] = back[parts:]
        send_y[pl.ds(2 * j + 1, parts, stride=rows), :] = back[:parts]
    y_start()

    def gradients_of(j):
        blocks = [recv_m[rows * c + 2 * j + half : rows * c + 2 * j + half + 1, :] for c in range(parts) for half in range(2)]
        fine_shifts(jnp.concatenate(blocks, axis=1), fine.at[j, LANES : 2 * LANES])
        for half in range(2):
            pads[half, 0:parts, :] = recv_p[pl.ds(2 * j + half, parts, stride=rows), :]
            pads[half, parts : 2 * parts, :] = zeros
        for n in range(2 * parts + 1):
            at = n // 2
            block = pads[n % 2, at : at + parts, :].astype(jnp.bfloat16)
            if n < 2 * parts:
                left[0:parts, LANES * n : LANES * (n + 1)] = block
            if n >= 1:
                left[parts : 2 * parts, LANES * (n - 1) : LANES * n] = block
        out = lax.dot_general(left[...], fine[j], NT, preferred_element_type=jnp.float32)
        for half in range(2):
            part = out[parts * half : parts * (half + 1)]
            send_g[pl.ds(2 * j + half, parts, stride=rows), :] = part[:, :LANES]
            send_f[pl.ds(2 * j + half, parts, stride=rows), :] = part[:, LANES:]

    p_recv()
    for j in range(own // 2):
        gradients_of(j)

    y_recv()
    gain = column(6)

    def conv_of(half):
        return recv_y[pl.ds(half, chans, stride=2), :] * fscale + gain * mixed_of(half)

    for half in range(2):
        peak = jnp.max(jnp.abs(dequant(0, half) * conv_of(half)), axis=0, keepdims=True)
        lm[half] = peak

    def push1(index, side):
        return pltpu.make_async_remote_copy(
            src_ref=lm.at[side],
            dst_ref=win1.at[CORES * index + core],
            send_sem=s1_send.at[CORES * index + side],
            recv_sem=s1_recv.at[CORES * index + core],
            device_id=chip_dev(off1[index], side),
            device_id_type=MESH,
        )

    def land1(index, side):
        return pltpu.make_async_remote_copy(
            src_ref=lm.at[core],
            dst_ref=win1.at[CORES * index + side],
            send_sem=s1_send.at[CORES * index + core],
            recv_sem=s1_recv.at[CORES * index + side],
            device_id=chip_dev(off1[index], side),
            device_id_type=MESH,
        )

    def sides(index, home):
        return (1 - core,) if index == home else tuple(range(CORES))

    for index in range(n1):
        for side in sides(index, self1):
            push1(index, side).start()
    win1[CORES * self1 + core] = lm[core]

    for j in range(own // 2, own):
        gradients_of(j)
    g_start()
    f_start()

    for index in range(n1):
        for side in sides(index, self1):
            land1(index, side).wait_recv()
    wide = jnp.max(win1[...], axis=0)
    wsend[0] = wide

    def push2(index, side):
        return pltpu.make_async_remote_copy(
            src_ref=wsend.at[0],
            dst_ref=win2.at[n2 * core + index],
            send_sem=s2_send.at[CORES * index + side],
            recv_sem=s2_recv.at[n2 * core + index],
            device_id=chip_dev(off2[index], side),
            device_id_type=MESH,
        )

    def land2(index, side):
        return pltpu.make_async_remote_copy(
            src_ref=wsend.at[0],
            dst_ref=win2.at[n2 * side + index],
            send_sem=s2_send.at[CORES * index + core],
            recv_sem=s2_recv.at[n2 * side + index],
            device_id=chip_dev(off2[index], side),
            device_id_type=MESH,
        )

    for index in range(n2):
        for side in sides(index, 0):
            push2(index, side).start()
    win2[n2 * core] = wide

    for half in range(2):
        gr_ref[0, :, LANES * half : LANES * (half + 1)] = (upstream(half) * conv_of(half)).astype(gr_ref.dtype)
    g_recv()
    for half in range(2):
        grad_mixed = recv_g[pl.ds(half, chans, stride=2), :] * fscale + gain * pulled_of(half)
        gr_ref[1, :, LANES * half : LANES * (half + 1)] = (grad_mixed * dequant(2, half)).astype(gr_ref.dtype)
        gr_ref[2, :, LANES * half : LANES * (half + 1)] = (grad_mixed * dequant(1, half)).astype(gr_ref.dtype)
    f_recv()
    reach = column(7)
    for half in range(2):
        lags = (me * (2 * LANES) + half * LANES + lax.broadcasted_iota(jnp.int32, (1, LANES), 1)).astype(jnp.float32)
        fg_ref[:, LANES * half : LANES * (half + 1)] = jnp.where(
            lags < reach, recv_f[pl.ds(half, chans, stride=2), :] * fscale, 0.0
        )

    for index in range(n2):
        for side in sides(index, 0):
            land2(index, side).wait_recv()
    for half in range(2):
        largest = jnp.max(win2[n2 * half : n2 * (half + 1)], axis=0)
        tm_ref[:, LANES * half : LANES * (half + 1)] = largest
        response = dequant(0, half) * conv_of(half)
        so_ref[:, LANES * half : LANES * (half + 1)] = (response / (largest + 1e-06)).astype(so_ref.dtype)

    for sent in (m_sent, p_sent, y_sent, g_sent, f_sent):
        sent()
    for index in range(n1):
        for side in sides(index, self1):
            push1(index, side).wait_send()
    for index in range(n2):
        for side in sides(index, 0):
            push2(index, side).wait_send()


def body(proj, scale_exp, filt, reach, skip, cotangent):
    groups, chans, span = proj.shape
    parts = lax.axis_size("ctx")
    chips = lax.axis_size("ch") // CORES
    seq = parts * span
    own = chans // parts
    divisors = jnp.array(REACH_DIVISORS, dtype=jnp.int32)
    class_ids = jnp.arange(len(REACH_DIVISORS), dtype=jnp.int32)
    reach_div = jnp.sum(jnp.where(reach[:, None] == class_ids[None, :], divisors[None, :], 0), axis=1)
    reach_len = seq // reach_div
    scaled = jnp.exp2(scale_exp.astype(jnp.float32))
    aux = jnp.concatenate(
        [jnp.transpose(scaled, (1, 0, 2)).reshape(chans, 2 * groups), skip[:, None], reach_len.astype(jnp.float32)[:, None]],
        axis=1,
    )
    n1, n2 = (len(offsets) for offsets in z_windows(chips))
    slab = pltpu.VMEM((2 * chans, LANES), jnp.float32)
    vmem = pl.BlockSpec(memory_space=pltpu.VMEM)
    scaled_out, token_max, gradients, filter_grad = pl.pallas_call(
        functools.partial(kernel, parts, chips, chans, seq),
        out_shape=(
            jax.ShapeDtypeStruct((chans, span), jnp.bfloat16),
            jax.ShapeDtypeStruct((1, span), jnp.float32),
            jax.ShapeDtypeStruct((groups, chans, span), jnp.bfloat16),
            jax.ShapeDtypeStruct((chans, span), jnp.float32),
        ),
        in_specs=[vmem, vmem, vmem, pl.BlockSpec(memory_space=pl.ANY)],
        out_specs=(vmem, vmem, vmem, vmem),
        scratch_shapes=[slab] * 10
        + [
            pltpu.VMEM((16, seq), jnp.bfloat16),
            pltpu.VMEM((16, seq), jnp.float32),
            pltpu.VMEM((own, 2 * LANES, seq), jnp.bfloat16),
            pltpu.VMEM((2, 2 * parts, LANES), jnp.float32),
            pltpu.VMEM((2 * parts, seq), jnp.bfloat16),
            slab,
            pltpu.VMEM((2, 1, LANES), jnp.float32),
            pltpu.VMEM((CORES * n1, 1, LANES), jnp.float32),
            pltpu.VMEM((1, 1, LANES), jnp.float32),
            pltpu.VMEM((CORES * n2, 1, LANES), jnp.float32),
            pltpu.SemaphoreType.DMA,
            pltpu.SemaphoreType.DMA((5, parts)),
            pltpu.SemaphoreType.DMA((5, parts)),
            pltpu.SemaphoreType.DMA((CORES * n1,)),
            pltpu.SemaphoreType.DMA((CORES * n1,)),
            pltpu.SemaphoreType.DMA((CORES * n2,)),
            pltpu.SemaphoreType.DMA((CORES * n2,)),
        ],
        compiler_params=pltpu.CompilerParams(
            collective_id=0, has_side_effects=True, vmem_limit_bytes=40 * 1024 * 1024
        ),
        name="hyena",
    )(aux, proj, cotangent, filt)
    return scaled_out, token_max.reshape(span), gradients, filter_grad


def solution(mesh):
    return jax.shard_map(
        body,
        mesh=mesh,
        in_specs=(
            P(None, "ch", "ctx"),
            P(None, "ch", "ctx"),
            P("ch", None),
            P("ch"),
            P("ch"),
            P("ch", "ctx"),
        ),
        out_specs=(P("ch", "ctx"), P("ctx"), P(None, "ch", "ctx"), P("ch", "ctx")),
        check_vma=False,
    )
```

```python
import functools
import math

import jax
import jax.numpy as jnp
from jax import lax
from jax.experimental import pallas as pl
from jax.experimental.pallas import tpu as pltpu
from jax.sharding import PartitionSpec as P

REACH_DIVISORS = (64, 32, 16, 4, 1)
MESH = pl.DeviceIdType.MESH
LANES = 128
CORES = 2
NT = (((1,), (1,)), ((), ()))


def z_windows(chips):
    if chips == 32:
        return tuple(range(-5, 6)), (0, -11, 11)
    return tuple(range(chips)), (0,)


def z_greetings(chips):
    if chips == 32:
        return tuple(range(-3, 4)), (3, 6)
    return tuple(range(chips)), ()


def fine_shifts(row, dst):
    width = row.shape[1]
    strip = pltpu.roll(jnp.broadcast_to(row, (8, width)), 0, 1, stride=1, stride_axis=0)
    lane = lax.broadcasted_iota(jnp.int32, (16, LANES), 1)
    sub = lax.broadcasted_iota(jnp.int32, (16, LANES), 0)
    for k in range(LANES // 16):
        low = strip if k == 0 else pltpu.roll(strip, 16 * k, 1)
        both = jnp.concatenate([low, pltpu.roll(strip, 16 * k + 8, 1)], axis=0)
        first = jnp.where(lane >= sub + 16 * k, both[:, :LANES], 0.0)
        dst[16 * k : 16 * k + 16, :LANES] = first.astype(jnp.bfloat16)
        dst[16 * k : 16 * k + 16, LANES:] = both[:, LANES:].astype(jnp.bfloat16)


def kernel(
    parts, chips, chans, seq,
    proj_hbm, scale_hbm, cot_hbm, filt, reach_hbm, skip_hbm,
    so_hbm, tm_hbm, gr_hbm, fg_hbm,
    so_ref, tm_ref, gr_ref, fg_ref,
    send_m, send_p, send_y, send_g, send_f,
    recv_m, recv_p, recv_y, recv_g, recv_f,
    proj, scale, cot, reach_row, skip_row, wide_rows, aux, response,
    taps_bf, taps, fine, pads, left, rev, turned,
    lm, win1, wsend, win2,
    in_sem, out_sem, ctx_send, ctx_recv, s1_send, s1_recv, s2_send, s2_recv, relay_sem,
):
    own = chans // parts
    rows = 2 * own
    fscale = 1.0 / math.sqrt(seq)
    me = lax.axis_index("ctx")
    ch = lax.axis_index("ch")
    zpos = ch // CORES
    core = ch % CORES
    off1, off2 = z_windows(chips)
    near, relays = z_greetings(chips)
    n1, n2 = len(off1), len(off2)
    self1 = off1.index(0)

    def peer_of(step):
        return lax.rem(me + step, parts)

    def chip_dev(offset, side):
        return {"ch": lax.rem(zpos + (offset + chips), chips) * CORES + side}

    barrier = pltpu.get_barrier_semaphore()

    def greet(step, carry):
        pl.semaphore_signal(barrier, inc=1, device_id={"ctx": peer_of(step)}, device_id_type=MESH)
        return carry

    lax.fori_loop(1, parts, greet, 0)
    greeted = parts - 1
    for offset in near:
        for side in (1 - core,) if offset == 0 else tuple(range(CORES)):
            pl.semaphore_signal(barrier, inc=1, device_id=chip_dev(offset, side), device_id_type=MESH)
            greeted += 1

    def relay_send(index):
        for offset in (-relays[index], relays[index]):
            pl.semaphore_signal(relay_sem.at[index], inc=1, device_id=chip_dev(offset, core), device_id_type=MESH)

    def relay_wait(index):
        pl.semaphore_wait(relay_sem.at[index], 2)

    per_tile = 16 // own
    tile = pl.multiple_of(me // per_tile * 16, 16)
    fetches = [
        pltpu.make_async_copy(src, dst, in_sem.at[index])
        for index, (src, dst) in enumerate(
            (
                (proj_hbm, proj),
                (scale_hbm, scale),
                (cot_hbm, cot),
                (reach_hbm, reach_row),
                (skip_hbm, skip_row),
                (filt.at[pl.ds(tile, 16), :], taps_bf),
            )
        )
    ]
    for fetch in fetches:
        fetch.start()
    for fetch in fetches[:-1]:
        fetch.wait()

    wide_rows[...] = jnp.zeros_like(wide_rows)
    for group in range(3):
        wide_rows[2 * group : 2 * group + 2, 0:chans] = jnp.exp2(scale[group].astype(jnp.float32))
    wide_rows[6:7, 0:chans] = skip_row[...]
    reach_len = jnp.zeros((1, chans), jnp.float32)
    for index, divisor in enumerate(REACH_DIVISORS):
        reach_len = jnp.where(reach_row[...] == index, float(seq // divisor), reach_len)
    wide_rows[7:8, 0:chans] = reach_len
    aux[...] = jnp.transpose(wide_rows[...])[0:chans]

    def column(index):
        return aux[:, index : index + 1]

    def dequant(group, half):
        values = proj[group, :, LANES * half : LANES * (half + 1)].astype(jnp.float32)
        return values * column(2 * group + half)

    def upstream(half):
        return cot[:, LANES * half : LANES * (half + 1)].astype(jnp.float32)

    def mixed_of(half):
        return (dequant(1, half) * dequant(2, half)).astype(jnp.bfloat16).astype(jnp.float32)

    def pulled_of(half):
        return (upstream(half) * dequant(0, half)).astype(jnp.bfloat16).astype(jnp.float32)

    for half in range(2):
        send_m[pl.ds(half, chans, stride=2), :] = mixed_of(half)
        send_p[pl.ds(half, chans, stride=2), :] = pulled_of(half)

    mine = pl.ds(pl.multiple_of(rows * me, rows), rows)

    def exchange(which, src, dst):
        def copy(step):
            peer = peer_of(step)
            return pltpu.make_async_remote_copy(
                src_ref=src.at[pl.ds(pl.multiple_of(rows * peer, rows), rows), :],
                dst_ref=dst.at[mine, :],
                send_sem=ctx_send.at[which, peer],
                recv_sem=ctx_recv.at[which, me],
                device_id={"ctx": peer},
                device_id_type=MESH,
            )

        def arrival(step):
            peer = peer_of(step)
            return pltpu.make_async_remote_copy(
                src_ref=src.at[mine, :],
                dst_ref=dst.at[pl.ds(pl.multiple_of(rows * peer, rows), rows), :],
                send_sem=ctx_send.at[which, me],
                recv_sem=ctx_recv.at[which, peer],
                device_id={"ctx": peer},
                device_id_type=MESH,
            )

        def start():
            def go(step, carry):
                copy(step).start()
                return carry

            lax.fori_loop(1, parts, go, 0)
            dst[mine, :] = src[mine, :]

        def wait_recv():
            def go(step, carry):
                arrival(step).wait_recv()
                return carry

            lax.fori_loop(1, parts, go, 0)

        def wait_send():
            def go(step, carry):
                copy(step).wait_send()
                return carry

            lax.fori_loop(1, parts, go, 0)

        return start, wait_recv, wait_send

    m_start, m_recv, m_sent = exchange(0, send_m, recv_m)
    p_start, p_recv, p_sent = exchange(1, send_p, recv_p)
    y_start, y_recv, y_sent = exchange(2, send_y, recv_y)
    g_start, g_recv, g_sent = exchange(3, send_g, recv_g)
    f_start, f_recv, f_sent = exchange(4, send_f, recv_f)

    pl.semaphore_wait(barrier, greeted)
    m_start()
    if relays:
        relay_send(0)
    p_start()

    fetches[-1].wait()
    taps[...] = taps_bf[...].astype(jnp.float32)
    lag = lax.broadcasted_iota(jnp.int32, (1, seq), 1).astype(jnp.float32)
    for j in range(own):
        row = taps[pl.ds(me % per_tile * own + j, 1), :]
        reach = aux[pl.ds(me * own + j, 1), :][:, 7:8]
        fine_shifts(jnp.where(lag < reach, row, 0.0), fine.at[j, 0:LANES])

    flip = (
        lax.broadcasted_iota(jnp.int32, (LANES, LANES), 0)
        + lax.broadcasted_iota(jnp.int32, (LANES, LANES), 1)
        == LANES - 1
    ).astype(jnp.float32).astype(jnp.bfloat16)

    def reverse(values):
        return jnp.dot(values, flip, preferred_element_type=jnp.float32)

    m_recv()
    rev[...] = reverse(recv_m[...].astype(jnp.bfloat16))
    zeros = jnp.zeros((parts, LANES), jnp.float32)
    for slot in range(2):
        pads[slot, 0:parts, :] = zeros
    for j in range(own):
        pads[0, parts : 2 * parts, :] = rev[pl.ds(2 * j + 1, parts, stride=rows), :]
        pads[1, parts : 2 * parts, :] = rev[pl.ds(2 * j, parts, stride=rows), :]
        for n in range(2 * parts + 1):
            at = parts - n // 2
            block = pads[n % 2, at : at + parts, :].astype(jnp.bfloat16)
            if n < 2 * parts:
                left[j, 0:parts, LANES * n : LANES * (n + 1)] = block
            if n >= 1:
                left[j, parts : 2 * parts, LANES * (n - 1) : LANES * n] = block
    for j in range(own):
        out = lax.dot_general(left[j], fine[j, 0:LANES, :], NT, preferred_element_type=jnp.float32)
        turned[pl.ds(2 * j, parts, stride=rows), :] = out[parts:]
        turned[pl.ds(2 * j + 1, parts, stride=rows), :] = out[:parts]
    whole = turned[...]
    top = whole.astype(jnp.bfloat16)
    rest = (whole - top.astype(jnp.float32)).astype(jnp.bfloat16)
    send_y[...] = reverse(top) + reverse(rest)
    y_start()
    if relays:
        relay_wait(0)
        relay_send(1)

    def gradients_of(j):
        blocks = [recv_m[rows * c + 2 * j + half : rows * c + 2 * j + half + 1, :] for c in range(parts) for half in range(2)]
        fine_shifts(jnp.concatenate(blocks, axis=1), fine.at[j, LANES : 2 * LANES])
        for half in range(2):
            pads[half, 0:parts, :] = recv_p[pl.ds(2 * j + half, parts, stride=rows), :]
            pads[half, parts : 2 * parts, :] = zeros
        for n in range(2 * parts + 1):
            at = n // 2
            block = pads[n % 2, at : at + parts, :].astype(jnp.bfloat16)
            if n < 2 * parts:
                left[j, 0:parts, LANES * n : LANES * (n + 1)] = block
            if n >= 1:
                left[j, parts : 2 * parts, LANES * (n - 1) : LANES * n] = block
        out = lax.dot_general(left[j], fine[j], NT, preferred_element_type=jnp.float32)
        for half in range(2):
            part = out[parts * half : parts * (half + 1)]
            send_g[pl.ds(2 * j + half, parts, stride=rows), :] = part[:, :LANES]
            send_f[pl.ds(2 * j + half, parts, stride=rows), :] = part[:, LANES:]

    p_recv()
    for j in range(own):
        gradients_of(j)

    y_recv()
    gain = column(6)

    def conv_of(half):
        return recv_y[pl.ds(half, chans, stride=2), :] * fscale + gain * mixed_of(half)

    for half in range(2):
        value = dequant(0, half) * conv_of(half)
        response[:, LANES * half : LANES * (half + 1)] = value
        lm[half] = jnp.max(jnp.abs(value), axis=0, keepdims=True)

    def push1(index, side):
        return pltpu.make_async_remote_copy(
            src_ref=lm.at[side],
            dst_ref=win1.at[CORES * index + core],
            send_sem=s1_send.at[CORES * index + side],
            recv_sem=s1_recv.at[CORES * index + core],
            device_id=chip_dev(off1[index], side),
            device_id_type=MESH,
        )

    def land1(index, side):
        return pltpu.make_async_remote_copy(
            src_ref=lm.at[core],
            dst_ref=win1.at[CORES * index + side],
            send_sem=s1_send.at[CORES * index + core],
            recv_sem=s1_recv.at[CORES * index + side],
            device_id=chip_dev(off1[index], side),
            device_id_type=MESH,
        )

    def sides(index, home):
        return (1 - core,) if index == home else tuple(range(CORES))

    for index in range(n1):
        for side in sides(index, self1):
            push1(index, side).start()
    win1[CORES * self1 + core] = lm[core]

    g_start()
    f_start()

    for index in range(n1):
        for side in sides(index, self1):
            land1(index, side).wait_recv()
    wide = jnp.max(win1[...], axis=0)
    wsend[0] = wide
    if relays:
        relay_wait(1)

    def push2(index, side):
        return pltpu.make_async_remote_copy(
            src_ref=wsend.at[0],
            dst_ref=win2.at[n2 * core + index],
            send_sem=s2_send.at[CORES * index + side],
            recv_sem=s2_recv.at[n2 * core + index],
            device_id=chip_dev(off2[index], side),
            device_id_type=MESH,
        )

    def land2(index, side):
        return pltpu.make_async_remote_copy(
            src_ref=wsend.at[0],
            dst_ref=win2.at[n2 * side + index],
            send_sem=s2_send.at[CORES * index + core],
            recv_sem=s2_recv.at[n2 * side + index],
            device_id=chip_dev(off2[index], side),
            device_id_type=MESH,
        )

    for index in range(n2):
        for side in sides(index, 0):
            push2(index, side).start()
    win2[n2 * core] = wide

    stores = [
        pltpu.make_async_copy(src, dst, out_sem.at[index])
        for index, (src, dst) in enumerate(
            ((gr_ref, gr_hbm), (fg_ref, fg_hbm), (tm_ref, tm_hbm), (so_ref, so_hbm))
        )
    ]
    for half in range(2):
        gr_ref[0, :, LANES * half : LANES * (half + 1)] = (upstream(half) * conv_of(half)).astype(gr_ref.dtype)
    g_recv()
    for half in range(2):
        grad_mixed = recv_g[pl.ds(half, chans, stride=2), :] * fscale + gain * pulled_of(half)
        gr_ref[1, :, LANES * half : LANES * (half + 1)] = (grad_mixed * dequant(2, half)).astype(gr_ref.dtype)
        gr_ref[2, :, LANES * half : LANES * (half + 1)] = (grad_mixed * dequant(1, half)).astype(gr_ref.dtype)
    stores[0].start()
    f_recv()
    reach = column(7)
    for half in range(2):
        lags = (me * (2 * LANES) + half * LANES + lax.broadcasted_iota(jnp.int32, (1, LANES), 1)).astype(jnp.float32)
        fg_ref[:, LANES * half : LANES * (half + 1)] = jnp.where(
            lags < reach, recv_f[pl.ds(half, chans, stride=2), :] * fscale, 0.0
        )

    stores[1].start()

    for index in range(n2):
        for side in sides(index, 0):
            land2(index, side).wait_recv()
    for half in range(2):
        largest = jnp.max(win2[n2 * half : n2 * (half + 1)], axis=0)
        tm_ref[:, LANES * half : LANES * (half + 1)] = largest
        value = response[:, LANES * half : LANES * (half + 1)]
        so_ref[:, LANES * half : LANES * (half + 1)] = (value / (largest + 1e-06)).astype(so_ref.dtype)

    stores[2].start()
    stores[3].start()

    for sent in (m_sent, p_sent, y_sent, g_sent, f_sent):
        sent()
    for index in range(n1):
        for side in sides(index, self1):
            push1(index, side).wait_send()
    for index in range(n2):
        for side in sides(index, 0):
            push2(index, side).wait_send()
    for store in stores:
        store.wait()


def write_out(*refs):
    count = len(refs) // 2
    sems = refs[-1]
    copies = [pltpu.make_async_copy(refs[index], refs[count + index], sems.at[index]) for index in range(count)]
    for copy in copies:
        copy.start()
    for copy in copies:
        copy.wait()


def body(proj, scale_exp, filt, reach, skip, cotangent):
    groups, chans, span = proj.shape
    parts = lax.axis_size("ctx")
    chips = lax.axis_size("ch") // CORES
    seq = parts * span
    own = chans // parts
    n1, n2 = (len(offsets) for offsets in z_windows(chips))
    slab = pltpu.VMEM((2 * chans, LANES), jnp.float32)
    hbm = pl.BlockSpec(memory_space=pltpu.HBM)
    shapes = (
        jax.ShapeDtypeStruct((chans, span), jnp.bfloat16),
        jax.ShapeDtypeStruct((1, span), jnp.float32),
        jax.ShapeDtypeStruct((groups, chans, span), jnp.bfloat16),
        jax.ShapeDtypeStruct((chans, span), jnp.float32),
    )
    results = pl.pallas_call(
        functools.partial(kernel, parts, chips, chans, seq),
        out_shape=shapes,
        in_specs=[hbm] * 6,
        out_specs=(hbm,) * 4,
        scratch_shapes=[pltpu.VMEM(shape.shape, shape.dtype) for shape in shapes]
        + [slab] * 10
        + [
            pltpu.VMEM((groups, chans, span), jnp.bfloat16),
            pltpu.VMEM((groups, 2, chans), jnp.int32),
            pltpu.VMEM((chans, span), jnp.bfloat16),
            pltpu.VMEM((1, chans), jnp.int32),
            pltpu.VMEM((1, chans), jnp.float32),
            pltpu.VMEM((8, LANES), jnp.float32),
            pltpu.VMEM((chans, 8), jnp.float32),
            pltpu.VMEM((chans, span), jnp.float32),
            pltpu.VMEM((16, seq), jnp.bfloat16),
            pltpu.VMEM((16, seq), jnp.float32),
            pltpu.VMEM((own, 2 * LANES, seq), jnp.bfloat16),
            pltpu.VMEM((2, 2 * parts, LANES), jnp.float32),
            pltpu.VMEM((own, 2 * parts, seq), jnp.bfloat16),
            slab,
            slab,
            pltpu.VMEM((2, 1, LANES), jnp.float32),
            pltpu.VMEM((CORES * n1, 1, LANES), jnp.float32),
            pltpu.VMEM((1, 1, LANES), jnp.float32),
            pltpu.VMEM((CORES * n2, 1, LANES), jnp.float32),
            pltpu.SemaphoreType.DMA((6,)),
            pltpu.SemaphoreType.DMA((4,)),
            pltpu.SemaphoreType.DMA((5, parts)),
            pltpu.SemaphoreType.DMA((5, parts)),
            pltpu.SemaphoreType.DMA((CORES * n1,)),
            pltpu.SemaphoreType.DMA((CORES * n1,)),
            pltpu.SemaphoreType.DMA((CORES * n2,)),
            pltpu.SemaphoreType.DMA((CORES * n2,)),
            pltpu.SemaphoreType.REGULAR((2,)),
        ],
        compiler_params=pltpu.CompilerParams(
            collective_id=0, has_side_effects=True, vmem_limit_bytes=58 * 1024 * 1024
        ),
        name="hyena",
    )(
        proj,
        jnp.transpose(scale_exp, (0, 2, 1)),
        cotangent,
        filt,
        reach.reshape(1, chans),
        skip.reshape(1, chans),
    )
    scaled_out, token_max, gradients, filter_grad = pl.pallas_call(
        write_out,
        out_shape=shapes,
        in_specs=[pl.BlockSpec(memory_space=pl.ANY)] * 4,
        out_specs=(hbm,) * 4,
        scratch_shapes=[pltpu.SemaphoreType.DMA((4,))],
        name="write_out",
    )(*results)
    return scaled_out, token_max.reshape(span), gradients, filter_grad


def solution(mesh):
    return jax.shard_map(
        body,
        mesh=mesh,
        in_specs=(
            P(None, "ch", "ctx"),
            P(None, "ch", "ctx"),
            P("ch", None),
            P("ch"),
            P("ch"),
            P("ch", "ctx"),
        ),
        out_specs=(P("ch", "ctx"), P("ctx"), P(None, "ch", "ctx"), P("ch", "ctx")),
        check_vma=False,
    )
```

```python
import functools
import math

import jax
import jax.numpy as jnp
from jax import lax
from jax.experimental import pallas as pl
from jax.experimental.pallas import tpu as pltpu
from jax.sharding import PartitionSpec as P

REACH_DIVISORS = (64, 32, 16, 4, 1)
MESH = pl.DeviceIdType.MESH
LANES = 128
CORES = 2
NT = (((1,), (1,)), ((), ()))


def z_greetings(chips):
    if chips == 32:
        return tuple(range(-4, 5)), (4, 8)
    return tuple(range(chips)), ()


def ctx_offsets(parts):
    if parts != 16:
        return None
    def hops(offset):
        return sum(min(part, 4 - part) for part in offset)
    return sorted(((a, b) for a in range(4) for b in range(4) if a or b), key=lambda offset: -hops(offset))


def fine_shifts(row, dst):
    width = row.shape[1]
    strip = pltpu.roll(jnp.broadcast_to(row, (8, width)), 0, 1, stride=1, stride_axis=0)
    lane = lax.broadcasted_iota(jnp.int32, (16, LANES), 1)
    sub = lax.broadcasted_iota(jnp.int32, (16, LANES), 0)
    for k in range(LANES // 16):
        low = strip if k == 0 else pltpu.roll(strip, 16 * k, 1)
        both = jnp.concatenate([low, pltpu.roll(strip, 16 * k + 8, 1)], axis=0)
        first = jnp.where(lane >= sub + 16 * k, both[:, :LANES], 0.0)
        dst[16 * k : 16 * k + 16, :LANES] = first.astype(jnp.bfloat16)
        dst[16 * k : 16 * k + 16, LANES:] = both[:, LANES:].astype(jnp.bfloat16)


def kernel(
    parts, chips, chans, seq,
    proj_hbm, scale_hbm, cot_hbm, filt, reach_hbm, skip_hbm,
    so_ref, tm_ref, gr_ref, fg_ref,
    send_m, send_p, send_y, send_g, send_f,
    recv_m, recv_p, recv_y, recv_g, recv_f,
    proj, scale, cot, reach_row, skip_row, wide_rows, aux, response,
    taps_bf, taps, fine, pads, left, rev, turned,
    lm, win, wide, other,
    in_sem, ctx_send, ctx_recv, z_send, z_recv, core_sem, relay_sem,
):
    own = chans // parts
    rows = 2 * own
    fscale = 1.0 / math.sqrt(seq)
    me = lax.axis_index("ctx")
    ch = lax.axis_index("ch")
    zpos = ch // CORES
    core = ch % CORES
    near, relays = z_greetings(chips)

    def peer_of(step):
        return lax.rem(me + step, parts)

    def chip_dev(offset, side):
        return {"ch": lax.rem(zpos + (offset + chips), chips) * CORES + side}

    barrier = pltpu.get_barrier_semaphore()

    offsets = ctx_offsets(parts)
    if offsets is None:
        far_first = [peer_of(step) for step in range(1, parts)]
    else:
        far_first = [lax.rem(me // 4 + a, 4) * 4 + lax.rem(me % 4 + b, 4) for a, b in offsets]
    for peer in far_first:
        pl.semaphore_signal(barrier, inc=1, device_id={"ctx": peer}, device_id_type=MESH)
    greeted = parts - 1
    for offset in near:
        for side in (1 - core,) if offset == 0 else tuple(range(CORES)):
            pl.semaphore_signal(barrier, inc=1, device_id=chip_dev(offset, side), device_id_type=MESH)
            greeted += 1

    def relay_send(index):
        for offset in (-relays[index], relays[index]):
            pl.semaphore_signal(relay_sem.at[index], inc=1, device_id=chip_dev(offset, core), device_id_type=MESH)

    def relay_wait(index):
        pl.semaphore_wait(relay_sem.at[index], 2)

    per_tile = 16 // own
    tile = pl.multiple_of(me // per_tile * 16, 16)
    fetches = [
        pltpu.make_async_copy(src, dst, in_sem.at[index])
        for index, (src, dst) in enumerate(
            (
                (proj_hbm, proj),
                (scale_hbm, scale),
                (cot_hbm, cot),
                (reach_hbm, reach_row),
                (skip_hbm, skip_row),
                (filt.at[pl.ds(tile, 16), :], taps_bf),
            )
        )
    ]
    for fetch in fetches:
        fetch.start()
    for fetch in fetches[:-1]:
        fetch.wait()

    wide_rows[...] = jnp.zeros_like(wide_rows)
    for group in range(3):
        wide_rows[2 * group : 2 * group + 2, 0:chans] = jnp.exp2(scale[group].astype(jnp.float32))
    wide_rows[6:7, 0:chans] = skip_row[...]
    reach_len = jnp.zeros((1, chans), jnp.float32)
    for index, divisor in enumerate(REACH_DIVISORS):
        reach_len = jnp.where(reach_row[...] == index, float(seq // divisor), reach_len)
    wide_rows[7:8, 0:chans] = reach_len
    aux[...] = jnp.transpose(wide_rows[...])[0:chans]

    def column(index):
        return aux[:, index : index + 1]

    def dequant(group, half):
        values = proj[group, :, LANES * half : LANES * (half + 1)].astype(jnp.float32)
        return values * column(2 * group + half)

    def upstream(half):
        return cot[:, LANES * half : LANES * (half + 1)].astype(jnp.float32)

    def mixed_of(half):
        return (dequant(1, half) * dequant(2, half)).astype(jnp.bfloat16).astype(jnp.float32)

    def pulled_of(half):
        return (upstream(half) * dequant(0, half)).astype(jnp.bfloat16).astype(jnp.float32)

    for half in range(2):
        send_m[pl.ds(half, chans, stride=2), :] = mixed_of(half)
        send_p[pl.ds(half, chans, stride=2), :] = pulled_of(half)

    mine = pl.ds(pl.multiple_of(rows * me, rows), rows)

    def exchange(which, src, dst, urgent=False):
        def copy(peer):
            return pltpu.make_async_remote_copy(
                src_ref=src.at[pl.ds(pl.multiple_of(rows * peer, rows), rows), :],
                dst_ref=dst.at[mine, :],
                send_sem=ctx_send.at[which, peer],
                recv_sem=ctx_recv.at[which, me],
                device_id={"ctx": peer},
                device_id_type=MESH,
            )

        def arrival(step):
            peer = peer_of(step)
            return pltpu.make_async_remote_copy(
                src_ref=src.at[mine, :],
                dst_ref=dst.at[pl.ds(pl.multiple_of(rows * peer, rows), rows), :],
                send_sem=ctx_send.at[which, me],
                recv_sem=ctx_recv.at[which, peer],
                device_id={"ctx": peer},
                device_id_type=MESH,
            )

        def start():
            def go(step, carry):
                copy(peer_of(step)).start()
                return carry

            if urgent:
                for peer in far_first:
                    copy(peer).start()
            else:
                lax.fori_loop(1, parts, go, 0)
            dst[mine, :] = src[mine, :]

        def wait_recv():
            def go(step, carry):
                arrival(step).wait_recv()
                return carry

            lax.fori_loop(1, parts, go, 0)

        def wait_send():
            def go(step, carry):
                copy(peer_of(step)).wait_send()
                return carry

            lax.fori_loop(1, parts, go, 0)

        return start, wait_recv, wait_send

    m_start, m_recv, m_sent = exchange(0, send_m, recv_m, urgent=True)
    p_start, p_recv, p_sent = exchange(1, send_p, recv_p)
    y_start, y_recv, y_sent = exchange(2, send_y, recv_y, urgent=True)
    g_start, g_recv, g_sent = exchange(3, send_g, recv_g)
    f_start, f_recv, f_sent = exchange(4, send_f, recv_f)

    pl.semaphore_wait(barrier, greeted)
    m_start()
    if relays:
        relay_send(0)
    p_start()

    fetches[-1].wait()
    taps[...] = taps_bf[...].astype(jnp.float32)
    lag = lax.broadcasted_iota(jnp.int32, (1, seq), 1).astype(jnp.float32)
    for j in range(own):
        row = taps[pl.ds(me % per_tile * own + j, 1), :]
        reach = aux[pl.ds(me * own + j, 1), :][:, 7:8]
        fine_shifts(jnp.where(lag < reach, row, 0.0), fine.at[j, 0:LANES])

    flip = (
        lax.broadcasted_iota(jnp.int32, (LANES, LANES), 0)
        + lax.broadcasted_iota(jnp.int32, (LANES, LANES), 1)
        == LANES - 1
    ).astype(jnp.float32).astype(jnp.bfloat16)

    def reverse(values):
        return jnp.dot(values, flip, preferred_element_type=jnp.float32)

    m_recv()
    if relays:
        relay_wait(0)
        relay_send(1)
    rev[...] = reverse(recv_m[...].astype(jnp.bfloat16))
    zeros = jnp.zeros((parts, LANES), jnp.float32)
    for slot in range(2):
        pads[slot, 0:parts, :] = zeros
    for j in range(own):
        pads[0, parts : 2 * parts, :] = rev[pl.ds(2 * j + 1, parts, stride=rows), :]
        pads[1, parts : 2 * parts, :] = rev[pl.ds(2 * j, parts, stride=rows), :]
        for n in range(2 * parts + 1):
            at = parts - n // 2
            block = pads[n % 2, at : at + parts, :].astype(jnp.bfloat16)
            if n < 2 * parts:
                left[j, 0:parts, LANES * n : LANES * (n + 1)] = block
            if n >= 1:
                left[j, parts : 2 * parts, LANES * (n - 1) : LANES * n] = block
    for j in range(own):
        out = lax.dot_general(left[j], fine[j, 0:LANES, :], NT, preferred_element_type=jnp.float32)
        turned[pl.ds(2 * j, parts, stride=rows), :] = out[parts:]
        turned[pl.ds(2 * j + 1, parts, stride=rows), :] = out[:parts]
    whole = turned[...]
    top = whole.astype(jnp.bfloat16)
    rest = (whole - top.astype(jnp.float32)).astype(jnp.bfloat16)
    send_y[...] = reverse(top) + reverse(rest)
    y_start()

    def gradients_of(j):
        blocks = [recv_m[rows * c + 2 * j + half : rows * c + 2 * j + half + 1, :] for c in range(parts) for half in range(2)]
        fine_shifts(jnp.concatenate(blocks, axis=1), fine.at[j, LANES : 2 * LANES])
        for half in range(2):
            pads[half, 0:parts, :] = recv_p[pl.ds(2 * j + half, parts, stride=rows), :]
            pads[half, parts : 2 * parts, :] = zeros
        for n in range(2 * parts + 1):
            at = n // 2
            block = pads[n % 2, at : at + parts, :].astype(jnp.bfloat16)
            if n < 2 * parts:
                left[j, 0:parts, LANES * n : LANES * (n + 1)] = block
            if n >= 1:
                left[j, parts : 2 * parts, LANES * (n - 1) : LANES * n] = block
        out = lax.dot_general(left[j], fine[j], NT, preferred_element_type=jnp.float32)
        for half in range(2):
            part = out[parts * half : parts * (half + 1)]
            send_g[pl.ds(2 * j + half, parts, stride=rows), :] = part[:, :LANES]
            send_f[pl.ds(2 * j + half, parts, stride=rows), :] = part[:, LANES:]

    p_recv()
    for j in range(own):
        gradients_of(j)

    y_recv()
    gain = column(6)

    def conv_of(half):
        return recv_y[pl.ds(half, chans, stride=2), :] * fscale + gain * mixed_of(half)

    for half in range(2):
        value = dequant(0, half) * conv_of(half)
        response[:, LANES * half : LANES * (half + 1)] = value
        lm[0, :, LANES * half : LANES * (half + 1)] = jnp.max(jnp.abs(value), axis=0, keepdims=True)

    def z_step(index):
        return chips // 2 + (index + 1) // 2 * (1 - 2 * (index % 2))

    def z_push(step):
        return pltpu.make_async_remote_copy(
            src_ref=lm.at[0],
            dst_ref=win.at[zpos],
            send_sem=z_send.at[step],
            recv_sem=z_recv.at[zpos],
            device_id=chip_dev(step, core),
            device_id_type=MESH,
        )

    def z_land(step):
        origin = lax.rem(zpos + step, chips)
        return pltpu.make_async_remote_copy(
            src_ref=lm.at[0],
            dst_ref=win.at[origin],
            send_sem=z_send.at[step],
            recv_sem=z_recv.at[origin],
            device_id=chip_dev(step, core),
            device_id_type=MESH,
        )

    def z_start(index, carry):
        z_push(z_step(index)).start()
        return carry

    def z_arrive(index, carry):
        z_land(z_step(chips - 2 - index)).wait_recv()
        return carry

    def z_sent(index, carry):
        z_push(z_step(index)).wait_send()
        return carry

    if relays:
        relay_wait(1)
    lax.fori_loop(0, chips - 1, z_start, 0)
    win[zpos] = lm[0]
    g_start()
    f_start()

    for half in range(2):
        gr_ref[0, :, LANES * half : LANES * (half + 1)] = (upstream(half) * conv_of(half)).astype(gr_ref.dtype)
    g_recv()
    for half in range(2):
        grad_mixed = recv_g[pl.ds(half, chans, stride=2), :] * fscale + gain * pulled_of(half)
        gr_ref[1, :, LANES * half : LANES * (half + 1)] = (grad_mixed * dequant(2, half)).astype(gr_ref.dtype)
        gr_ref[2, :, LANES * half : LANES * (half + 1)] = (grad_mixed * dequant(1, half)).astype(gr_ref.dtype)
    f_recv()
    reach = column(7)
    for half in range(2):
        lags = (me * (2 * LANES) + half * LANES + lax.broadcasted_iota(jnp.int32, (1, LANES), 1)).astype(jnp.float32)
        fg_ref[:, LANES * half : LANES * (half + 1)] = jnp.where(
            lags < reach, recv_f[pl.ds(half, chans, stride=2), :] * fscale, 0.0
        )


    lax.fori_loop(0, chips - 1, z_arrive, 0)
    wide[0] = jnp.max(win[...], axis=0)
    swap = pltpu.make_async_remote_copy(
        src_ref=wide.at[0],
        dst_ref=other.at[0],
        send_sem=core_sem.at[0],
        recv_sem=core_sem.at[1],
        device_id=chip_dev(0, 1 - core),
        device_id_type=MESH,
    )
    swap.start()
    swap.wait_recv()
    largest = jnp.maximum(wide[0], other[0])
    tm_ref[...] = largest
    so_ref[...] = (response[...] / (largest + 1e-06)).astype(so_ref.dtype)

    for sent in (m_sent, p_sent, y_sent, g_sent, f_sent):
        sent()
    lax.fori_loop(0, chips - 1, z_sent, 0)
    swap.wait_send()


def write_out(*refs):
    count = len(refs) // 2
    sems = refs[-1]
    copies = [pltpu.make_async_copy(refs[index], refs[count + index], sems.at[index]) for index in range(count)]
    for copy in copies:
        copy.start()
    for copy in copies:
        copy.wait()


def body(proj, scale_exp, filt, reach, skip, cotangent):
    groups, chans, span = proj.shape
    parts = lax.axis_size("ctx")
    chips = lax.axis_size("ch") // CORES
    seq = parts * span
    own = chans // parts
    slab = pltpu.VMEM((2 * chans, LANES), jnp.float32)
    hbm = pl.BlockSpec(memory_space=pltpu.HBM)
    vmem = pl.BlockSpec(memory_space=pltpu.VMEM)
    shapes = (
        jax.ShapeDtypeStruct((chans, span), jnp.bfloat16),
        jax.ShapeDtypeStruct((1, span), jnp.float32),
        jax.ShapeDtypeStruct((groups, chans, span), jnp.bfloat16),
        jax.ShapeDtypeStruct((chans, span), jnp.float32),
    )
    results = pl.pallas_call(
        functools.partial(kernel, parts, chips, chans, seq),
        out_shape=shapes,
        in_specs=[hbm] * 6,
        out_specs=(vmem,) * 4,
        scratch_shapes=[slab] * 10
        + [
            pltpu.VMEM((groups, chans, span), jnp.bfloat16),
            pltpu.VMEM((groups, 2, chans), jnp.int32),
            pltpu.VMEM((chans, span), jnp.bfloat16),
            pltpu.VMEM((1, chans), jnp.int32),
            pltpu.VMEM((1, chans), jnp.float32),
            pltpu.VMEM((8, LANES), jnp.float32),
            pltpu.VMEM((chans, 8), jnp.float32),
            pltpu.VMEM((chans, span), jnp.float32),
            pltpu.VMEM((16, seq), jnp.bfloat16),
            pltpu.VMEM((16, seq), jnp.float32),
            pltpu.VMEM((own, 2 * LANES, seq), jnp.bfloat16),
            pltpu.VMEM((2, 2 * parts, LANES), jnp.float32),
            pltpu.VMEM((own, 2 * parts, seq), jnp.bfloat16),
            slab,
            slab,
            pltpu.VMEM((1, 1, span), jnp.float32),
            pltpu.VMEM((chips, 1, span), jnp.float32),
            pltpu.VMEM((1, 1, span), jnp.float32),
            pltpu.VMEM((1, 1, span), jnp.float32),
            pltpu.SemaphoreType.DMA((6,)),
            pltpu.SemaphoreType.DMA((5, parts)),
            pltpu.SemaphoreType.DMA((5, parts)),
            pltpu.SemaphoreType.DMA((chips,)),
            pltpu.SemaphoreType.DMA((chips,)),
            pltpu.SemaphoreType.DMA((2,)),
            pltpu.SemaphoreType.REGULAR((2,)),
        ],
        compiler_params=pltpu.CompilerParams(
            collective_id=0, has_side_effects=True, vmem_limit_bytes=40 * 1024 * 1024
        ),
        name="hyena",
    )(
        *(
            pltpu.with_memory_space_constraint(arg, pltpu.HBM)
            for arg in (
                proj,
                jnp.transpose(scale_exp, (0, 2, 1)),
                cotangent,
                filt,
                reach.reshape(1, chans),
                skip.reshape(1, chans),
            )
        )
    )
    scaled_out, token_max, gradients, filter_grad = pl.pallas_call(
        write_out,
        out_shape=shapes,
        in_specs=[pl.BlockSpec(memory_space=pl.ANY)] * 4,
        out_specs=(hbm,) * 4,
        scratch_shapes=[pltpu.SemaphoreType.DMA((4,))],
        compiler_params=pltpu.CompilerParams(vmem_limit_bytes=1024 * 1024),
        name="write_out",
    )(*results)
    return scaled_out, token_max.reshape(span), gradients, filter_grad


def solution(mesh):
    return jax.shard_map(
        body,
        mesh=mesh,
        in_specs=(
            P(None, "ch", "ctx"),
            P(None, "ch", "ctx"),
            P("ch", None),
            P("ch"),
            P("ch"),
            P("ch", "ctx"),
        ),
        out_specs=(P("ch", "ctx"), P("ctx"), P(None, "ch", "ctx"), P("ch", "ctx")),
        check_vma=False,
    )
```

```python
import functools
import math

import jax
import jax.numpy as jnp
from jax import lax
from jax.experimental import pallas as pl
from jax.experimental.pallas import tpu as pltpu
from jax.sharding import PartitionSpec as P

REACH_DIVISORS = (64, 32, 16, 4, 1)
MESH = pl.DeviceIdType.MESH
LANES = 128
CORES = 2
NT = (((1,), (1,)), ((), ()))


def z_greetings(chips):
    if chips == 32:
        return tuple(range(-4, 5)), (4, 8)
    return tuple(range(chips)), ()


def ctx_offsets(parts):
    if parts != 16:
        return None
    def hops(offset):
        return sum(min(part, 4 - part) for part in offset)
    return sorted(((a, b) for a in range(4) for b in range(4) if a or b), key=lambda offset: -hops(offset))


def fine_shifts(row, dst, backward=False):
    width = row.shape[1]
    strip = pltpu.roll(jnp.broadcast_to(row, (8, width)), 0, 1, stride=1, stride_axis=0)
    lane = lax.broadcasted_iota(jnp.int32, (16, LANES), 1)
    sub = lax.broadcasted_iota(jnp.int32, (16, LANES), 0)
    if backward:
        strip = jnp.dot(exchange_matrix(8), strip.astype(jnp.bfloat16), preferred_element_type=jnp.float32)
    for k in range(LANES // 16):
        if backward:
            first, second, shift = LANES - 8 - 16 * k, LANES - 16 - 16 * k, LANES - 1 - 16 * k - sub
        else:
            first, second, shift = 16 * k, 16 * k + 8, 16 * k + sub
        halves = [strip if by == 0 else pltpu.roll(strip, by, 1) for by in (first, second)]
        both = jnp.concatenate(halves, axis=0)
        start = jnp.where(lane >= shift, both[:, :LANES], 0.0)
        dst[16 * k : 16 * k + 16, :LANES] = start.astype(jnp.bfloat16)
        dst[16 * k : 16 * k + 16, LANES:] = both[:, LANES:].astype(jnp.bfloat16)


def exchange_matrix(size):
    total = lax.broadcasted_iota(jnp.int32, (size, size), 0) + lax.broadcasted_iota(jnp.int32, (size, size), 1)
    return (total == size - 1).astype(jnp.float32).astype(jnp.bfloat16)


def kernel(
    parts, chips, chans, seq,
    proj_hbm, scale_hbm, cot_hbm, filt, reach_hbm, skip_hbm,
    so_ref, tm_ref, gr_ref, fg_ref,
    send_m, send_p, send_y, send_g, send_f,
    recv_m, recv_p, recv_y, recv_g, recv_f,
    proj, scale, cot, reach_row, skip_row, wide_rows, aux, response, factor, offset_term,
    taps_bf, taps, fine, pads, left, ahead, turned,
    lm, win, wide, other,
    in_sem, ctx_send, ctx_recv, z_send, z_recv, core_sem, relay_sem,
):
    own = chans // parts
    rows = 2 * own
    fscale = 1.0 / math.sqrt(seq)
    me = lax.axis_index("ctx")
    ch = lax.axis_index("ch")
    zpos = ch // CORES
    core = ch % CORES
    near, relays = z_greetings(chips)

    def peer_of(step):
        return lax.rem(me + step, parts)

    def chip_dev(offset, side):
        return {"ch": lax.rem(zpos + (offset + chips), chips) * CORES + side}

    barrier = pltpu.get_barrier_semaphore()

    offsets = ctx_offsets(parts)
    if offsets is None:
        far_first = [peer_of(step) for step in range(1, parts)]
    else:
        far_first = [lax.rem(me // 4 + a, 4) * 4 + lax.rem(me % 4 + b, 4) for a, b in offsets]
    for peer in far_first:
        pl.semaphore_signal(barrier, inc=1, device_id={"ctx": peer}, device_id_type=MESH)
    greeted = parts - 1
    for offset in near:
        for side in (1 - core,) if offset == 0 else tuple(range(CORES)):
            pl.semaphore_signal(barrier, inc=1, device_id=chip_dev(offset, side), device_id_type=MESH)
            greeted += 1

    def relay_send(index):
        for offset in (-relays[index], relays[index]):
            pl.semaphore_signal(relay_sem.at[index], inc=1, device_id=chip_dev(offset, core), device_id_type=MESH)

    def relay_wait(index):
        pl.semaphore_wait(relay_sem.at[index], 2)

    per_tile = 16 // own
    tile = pl.multiple_of(me // per_tile * 16, 16)
    fetches = [
        pltpu.make_async_copy(src, dst, in_sem.at[index])
        for index, (src, dst) in enumerate(
            (
                (proj_hbm, proj),
                (scale_hbm, scale),
                (cot_hbm, cot),
                (reach_hbm, reach_row),
                (skip_hbm, skip_row),
                (filt.at[pl.ds(tile, 16), :], taps_bf),
            )
        )
    ]
    for fetch in fetches:
        fetch.start()
    for fetch in fetches[:-1]:
        fetch.wait()

    wide_rows[...] = jnp.zeros_like(wide_rows)
    for group in range(3):
        wide_rows[2 * group : 2 * group + 2, 0:chans] = jnp.exp2(scale[group].astype(jnp.float32))
    wide_rows[6:7, 0:chans] = skip_row[...]
    reach_len = jnp.zeros((1, chans), jnp.float32)
    for index, divisor in enumerate(REACH_DIVISORS):
        reach_len = jnp.where(reach_row[...] == index, float(seq // divisor), reach_len)
    wide_rows[7:8, 0:chans] = reach_len
    aux[...] = jnp.transpose(wide_rows[...])[0:chans]

    def column(index):
        return aux[:, index : index + 1]

    def dequant(group, half):
        values = proj[group, :, LANES * half : LANES * (half + 1)].astype(jnp.float32)
        return values * column(2 * group + half)

    def upstream(half):
        return cot[:, LANES * half : LANES * (half + 1)].astype(jnp.float32)

    def mixed_of(half):
        return (dequant(1, half) * dequant(2, half)).astype(jnp.bfloat16).astype(jnp.float32)

    def pulled_of(half):
        return (upstream(half) * dequant(0, half)).astype(jnp.bfloat16).astype(jnp.float32)

    flip = exchange_matrix(LANES)

    def reverse(values):
        return jnp.dot(values, flip, preferred_element_type=jnp.float32)

    def reverse_wide(values):
        top = values.astype(jnp.bfloat16)
        rest = (values - top.astype(jnp.float32)).astype(jnp.bfloat16)
        return reverse(top) + reverse(rest)

    for half in range(2):
        send_m[pl.ds(half, chans, stride=2), :] = reverse(mixed_of(half).astype(jnp.bfloat16))
        send_p[pl.ds(half, chans, stride=2), :] = pulled_of(half)

    mine = pl.ds(pl.multiple_of(rows * me, rows), rows)

    def exchange(which, src, dst, urgent=False):
        def copy(peer):
            return pltpu.make_async_remote_copy(
                src_ref=src.at[pl.ds(pl.multiple_of(rows * peer, rows), rows), :],
                dst_ref=dst.at[mine, :],
                send_sem=ctx_send.at[which, peer],
                recv_sem=ctx_recv.at[which, me],
                device_id={"ctx": peer},
                device_id_type=MESH,
            )

        def arrival(peer):
            return pltpu.make_async_remote_copy(
                src_ref=src.at[mine, :],
                dst_ref=dst.at[pl.ds(pl.multiple_of(rows * peer, rows), rows), :],
                send_sem=ctx_send.at[which, me],
                recv_sem=ctx_recv.at[which, peer],
                device_id={"ctx": peer},
                device_id_type=MESH,
            )

        def start():
            def go(step, carry):
                copy(peer_of(step)).start()
                return carry

            if urgent:
                for peer in far_first:
                    copy(peer).start()
            else:
                lax.fori_loop(1, parts, go, 0)
            dst[mine, :] = src[mine, :]

        def wait_recv():
            def go(step, carry):
                arrival(peer_of(step)).wait_recv()
                return carry

            if urgent:
                for peer in reversed(far_first):
                    arrival(peer).wait_recv()
            else:
                lax.fori_loop(1, parts, go, 0)

        def wait_send():
            def go(step, carry):
                copy(peer_of(step)).wait_send()
                return carry

            lax.fori_loop(1, parts, go, 0)

        return start, wait_recv, wait_send

    m_start, m_recv, m_sent = exchange(0, send_m, recv_m, urgent=True)
    p_start, p_recv, p_sent = exchange(1, send_p, recv_p)
    y_start, y_recv, y_sent = exchange(2, send_y, recv_y, urgent=True)
    g_start, g_recv, g_sent = exchange(3, send_g, recv_g)
    f_start, f_recv, f_sent = exchange(4, send_f, recv_f)

    pl.semaphore_wait(barrier, greeted)
    m_start()
    if relays:
        relay_send(0)

    fetches[-1].wait()
    taps[...] = taps_bf[...].astype(jnp.float32)
    lag = lax.broadcasted_iota(jnp.int32, (1, seq), 1).astype(jnp.float32)
    for j in range(own):
        row = taps[pl.ds(me % per_tile * own + j, 1), :]
        reach = aux[pl.ds(me * own + j, 1), :][:, 7:8]
        fine_shifts(jnp.where(lag < reach, row, 0.0), fine.at[j, 0:LANES], backward=True)

    p_start()
    if relays:
        relay_wait(0)
        relay_send(1)

    m_recv()
    zeros = jnp.zeros((parts, LANES), jnp.float32)
    for slot in range(2):
        pads[slot, 0:parts, :] = zeros
    for j in range(own):
        pads[0, parts : 2 * parts, :] = recv_m[pl.ds(2 * j + 1, parts, stride=rows), :]
        pads[1, parts : 2 * parts, :] = recv_m[pl.ds(2 * j, parts, stride=rows), :]
        for n in range(2 * parts + 1):
            at = parts - n // 2
            block = pads[n % 2, at : at + parts, :].astype(jnp.bfloat16)
            if n < 2 * parts:
                left[j, 0:parts, LANES * n : LANES * (n + 1)] = block
            if n >= 1:
                left[j, parts : 2 * parts, LANES * (n - 1) : LANES * n] = block
    for j in range(own):
        out = lax.dot_general(left[j], fine[j, 0:LANES, :], NT, preferred_element_type=jnp.float32)
        send_y[pl.ds(2 * j, parts, stride=rows), :] = out[parts:]
        send_y[pl.ds(2 * j + 1, parts, stride=rows), :] = out[:parts]
    y_start()

    def gradients_of(j):
        blocks = [ahead[rows * c + 2 * j + half : rows * c + 2 * j + half + 1, :] for c in range(parts) for half in range(2)]
        fine_shifts(jnp.concatenate(blocks, axis=1), fine.at[j, LANES : 2 * LANES])
        for half in range(2):
            pads[half, 0:parts, :] = recv_p[pl.ds(2 * j + half, parts, stride=rows), :]
            pads[half, parts : 2 * parts, :] = zeros
        for n in range(2 * parts + 1):
            at = n // 2
            block = pads[n % 2, at : at + parts, :].astype(jnp.bfloat16)
            if n < 2 * parts:
                left[j, 0:parts, LANES * n : LANES * (n + 1)] = block
            if n >= 1:
                left[j, parts : 2 * parts, LANES * (n - 1) : LANES * n] = block
        out = lax.dot_general(left[j], fine[j], NT, preferred_element_type=jnp.float32)
        for half in range(2):
            part = out[parts * half : parts * (half + 1)]
            turned[pl.ds(2 * j + half, parts, stride=rows), :] = part[:, :LANES]
            send_f[pl.ds(2 * j + half, parts, stride=rows), :] = part[:, LANES:]

    ahead[...] = reverse(recv_m[...].astype(jnp.bfloat16))
    gain = column(6)
    for half in range(2):
        query = dequant(0, half)
        factor[:, LANES * half : LANES * (half + 1)] = query * fscale
        offset_term[:, LANES * half : LANES * (half + 1)] = query * (gain * mixed_of(half))
    p_recv()
    for j in range(own // 2):
        gradients_of(j)

    y_recv()
    for half in range(2):
        block = slice(LANES * half, LANES * (half + 1))
        value = factor[:, block] * recv_y[pl.ds(half, chans, stride=2), :] + offset_term[:, block]
        response[:, block] = value
        lm[0, :, block] = jnp.max(jnp.abs(value), axis=0, keepdims=True)

    def conv_of(half):
        return recv_y[pl.ds(half, chans, stride=2), :] * fscale + gain * mixed_of(half)

    def z_step(index):
        return chips // 2 + (index + 1) // 2 * (1 - 2 * (index % 2))

    def z_push(step):
        return pltpu.make_async_remote_copy(
            src_ref=lm.at[0],
            dst_ref=win.at[zpos],
            send_sem=z_send.at[step],
            recv_sem=z_recv.at[zpos],
            device_id=chip_dev(step, core),
            device_id_type=MESH,
        )

    def z_land(step):
        origin = lax.rem(zpos + step, chips)
        return pltpu.make_async_remote_copy(
            src_ref=lm.at[0],
            dst_ref=win.at[origin],
            send_sem=z_send.at[step],
            recv_sem=z_recv.at[origin],
            device_id=chip_dev(step, core),
            device_id_type=MESH,
        )

    def z_start(index, carry):
        z_push(z_step(index)).start()
        return carry

    def z_arrive(index, carry):
        z_land(z_step(chips - 2 - index)).wait_recv()
        return carry

    def z_sent(index, carry):
        z_push(z_step(index)).wait_send()
        return carry

    if relays:
        relay_wait(1)
    lax.fori_loop(0, chips - 1, z_start, 0)
    win[zpos] = lm[0]
    for j in range(own // 2, own):
        gradients_of(j)
    send_g[...] = reverse_wide(turned[...])
    g_start()
    f_start()

    for half in range(2):
        gr_ref[0, :, LANES * half : LANES * (half + 1)] = (upstream(half) * conv_of(half)).astype(gr_ref.dtype)
    g_recv()
    for half in range(2):
        grad_mixed = recv_g[pl.ds(half, chans, stride=2), :] * fscale + gain * pulled_of(half)
        gr_ref[1, :, LANES * half : LANES * (half + 1)] = (grad_mixed * dequant(2, half)).astype(gr_ref.dtype)
        gr_ref[2, :, LANES * half : LANES * (half + 1)] = (grad_mixed * dequant(1, half)).astype(gr_ref.dtype)
    f_recv()
    reach = column(7)
    for half in range(2):
        lags = (me * (2 * LANES) + half * LANES + lax.broadcasted_iota(jnp.int32, (1, LANES), 1)).astype(jnp.float32)
        fg_ref[:, LANES * half : LANES * (half + 1)] = jnp.where(
            lags < reach, recv_f[pl.ds(half, chans, stride=2), :] * fscale, 0.0
        )


    lax.fori_loop(0, chips - 1, z_arrive, 0)
    wide[0] = jnp.max(win[...], axis=0)
    swap = pltpu.make_async_remote_copy(
        src_ref=wide.at[0],
        dst_ref=other.at[0],
        send_sem=core_sem.at[0],
        recv_sem=core_sem.at[1],
        device_id=chip_dev(0, 1 - core),
        device_id_type=MESH,
    )
    swap.start()
    swap.wait_recv()
    largest = jnp.maximum(wide[0], other[0])
    tm_ref[...] = largest
    so_ref[...] = (response[...] / (largest + 1e-06)).astype(so_ref.dtype)

    for sent in (m_sent, p_sent, y_sent, g_sent, f_sent):
        sent()
    lax.fori_loop(0, chips - 1, z_sent, 0)
    swap.wait_send()


def write_out(*refs):
    count = len(refs) // 2
    sems = refs[-1]
    copies = [pltpu.make_async_copy(refs[index], refs[count + index], sems.at[index]) for index in range(count)]
    for copy in copies:
        copy.start()
    for copy in copies:
        copy.wait()


def body(proj, scale_exp, filt, reach, skip, cotangent):
    groups, chans, span = proj.shape
    parts = lax.axis_size("ctx")
    chips = lax.axis_size("ch") // CORES
    seq = parts * span
    own = chans // parts
    slab = pltpu.VMEM((2 * chans, LANES), jnp.float32)
    hbm = pl.BlockSpec(memory_space=pltpu.HBM)
    vmem = pl.BlockSpec(memory_space=pltpu.VMEM)
    shapes = (
        jax.ShapeDtypeStruct((chans, span), jnp.bfloat16),
        jax.ShapeDtypeStruct((1, span), jnp.float32),
        jax.ShapeDtypeStruct((groups, chans, span), jnp.bfloat16),
        jax.ShapeDtypeStruct((chans, span), jnp.float32),
    )
    results = pl.pallas_call(
        functools.partial(kernel, parts, chips, chans, seq),
        out_shape=shapes,
        in_specs=[hbm] * 6,
        out_specs=(vmem,) * 4,
        scratch_shapes=[slab] * 10
        + [
            pltpu.VMEM((groups, chans, span), jnp.bfloat16),
            pltpu.VMEM((groups, 2, chans), jnp.int32),
            pltpu.VMEM((chans, span), jnp.bfloat16),
            pltpu.VMEM((1, chans), jnp.int32),
            pltpu.VMEM((1, chans), jnp.float32),
            pltpu.VMEM((8, LANES), jnp.float32),
            pltpu.VMEM((chans, 8), jnp.float32),
            pltpu.VMEM((chans, span), jnp.float32),
            pltpu.VMEM((chans, span), jnp.float32),
            pltpu.VMEM((chans, span), jnp.float32),
            pltpu.VMEM((16, seq), jnp.bfloat16),
            pltpu.VMEM((16, seq), jnp.float32),
            pltpu.VMEM((own, 2 * LANES, seq), jnp.bfloat16),
            pltpu.VMEM((2, 2 * parts, LANES), jnp.float32),
            pltpu.VMEM((own, 2 * parts, seq), jnp.bfloat16),
            slab,
            slab,
            pltpu.VMEM((1, 1, span), jnp.float32),
            pltpu.VMEM((chips, 1, span), jnp.float32),
            pltpu.VMEM((1, 1, span), jnp.float32),
            pltpu.VMEM((1, 1, span), jnp.float32),
            pltpu.SemaphoreType.DMA((6,)),
            pltpu.SemaphoreType.DMA((5, parts)),
            pltpu.SemaphoreType.DMA((5, parts)),
            pltpu.SemaphoreType.DMA((chips,)),
            pltpu.SemaphoreType.DMA((chips,)),
            pltpu.SemaphoreType.DMA((2,)),
            pltpu.SemaphoreType.REGULAR((2,)),
        ],
        compiler_params=pltpu.CompilerParams(
            collective_id=0, has_side_effects=True, vmem_limit_bytes=40 * 1024 * 1024
        ),
        name="hyena",
    )(
        *(
            pltpu.with_memory_space_constraint(arg, pltpu.HBM)
            for arg in (
                proj,
                jnp.transpose(scale_exp, (0, 2, 1)),
                cotangent,
                filt,
                reach.reshape(1, chans),
                skip.reshape(1, chans),
            )
        )
    )
    scaled_out, token_max, gradients, filter_grad = pl.pallas_call(
        write_out,
        out_shape=shapes,
        in_specs=[pl.BlockSpec(memory_space=pl.ANY)] * 4,
        out_specs=(hbm,) * 4,
        scratch_shapes=[pltpu.SemaphoreType.DMA((4,))],
        compiler_params=pltpu.CompilerParams(vmem_limit_bytes=1024 * 1024),
        name="write_out",
    )(*results)
    return scaled_out, token_max.reshape(span), gradients, filter_grad


def solution(mesh):
    return jax.shard_map(
        body,
        mesh=mesh,
        in_specs=(
            P(None, "ch", "ctx"),
            P(None, "ch", "ctx"),
            P("ch", None),
            P("ch"),
            P("ch"),
            P("ch", "ctx"),
        ),
        out_specs=(P("ch", "ctx"), P("ctx"), P(None, "ch", "ctx"), P("ch", "ctx")),
        check_vma=False,
    )
```

```python
import functools
import math

import jax
import jax.numpy as jnp
from jax import lax
from jax.experimental import pallas as pl
from jax.experimental.pallas import tpu as pltpu
from jax.sharding import PartitionSpec as P

REACH_DIVISORS = (64, 32, 16, 4, 1)
MESH = pl.DeviceIdType.MESH
LANES = 128
CORES = 2


def z_greetings(chips):
    if chips == 32:
        return tuple(range(-4, 5)), (4, 8)
    return tuple(range(chips)), ()


def ctx_hops(offset):
    return sum(min(part, 4 - part) for part in offset)


def ctx_offsets(parts):
    if parts != 16:
        return None
    return sorted(((a, b) for a in range(4) for b in range(4) if a or b), key=lambda offset: -ctx_hops(offset))


def fine_shifts(row, dst):
    width = row.shape[1]
    total = width + LANES
    padded = jnp.concatenate([jnp.zeros((1, LANES), jnp.float32), row], axis=1)
    strip = pltpu.roll(jnp.broadcast_to(padded, (8, total)), 0, 1, stride=1, stride_axis=0)
    strip = jnp.dot(exchange_matrix(8), strip.astype(jnp.bfloat16), preferred_element_type=jnp.float32)
    for k in range(LANES // 16):
        halves = [pltpu.roll(strip, total - by, 1) for by in (16 * k + 8, 16 * k + 16)]
        both = jnp.concatenate(halves, axis=0).astype(jnp.bfloat16)
        for n in range(width // LANES):
            dst[LANES * n + 16 * k : LANES * n + 16 * k + 16, :] = both[:, LANES * n : LANES * (n + 1)]


def exchange_matrix(size):
    total = lax.broadcasted_iota(jnp.int32, (size, size), 0) + lax.broadcasted_iota(jnp.int32, (size, size), 1)
    return (total == size - 1).astype(jnp.float32).astype(jnp.bfloat16)


def kernel(
    parts, chips, chans, seq,
    proj_hbm, scale_hbm, cot_hbm, filt, reach_hbm, skip_hbm,
    so_ref, tm_ref, gr_ref, fg_ref,
    send_m, send_p, send_y, send_g, send_f,
    recv_m, recv_p, recv_y, recv_g, recv_f,
    proj, scale, cot, reach_row, skip_row, wide_rows, aux, response, factor, offset_term,
    taps_bf, taps, fine, pads, left, ahead, turned_g, turned_f,
    lm, win, wide, other,
    in_sem, ctx_send, ctx_recv, z_send, z_recv, core_sem, relay_sem,
):
    own = chans // parts
    rows = 2 * own
    fscale = 1.0 / math.sqrt(seq)
    me = lax.axis_index("ctx")
    ch = lax.axis_index("ch")
    zpos = ch // CORES
    core = ch % CORES
    near, relays = z_greetings(chips)

    def peer_of(step):
        return lax.rem(me + step, parts)

    def chip_dev(offset, side):
        return {"ch": lax.rem(zpos + (offset + chips), chips) * CORES + side}

    barrier = pltpu.get_barrier_semaphore()

    offsets = ctx_offsets(parts)
    if offsets is None:
        far_first = [peer_of(step) for step in range(1, parts)]
        targets = [(0, {"ctx": peer}) for peer in far_first]
    else:
        far_first = [lax.rem(me // 4 + a, 4) * 4 + lax.rem(me % 4 + b, 4) for a, b in offsets]
        targets = [(ctx_hops(offset), {"ctx": peer}) for offset, peer in zip(offsets, far_first)]
    for offset in near:
        for side in (1 - core,) if offset == 0 else tuple(range(CORES)):
            targets.append((abs(offset), chip_dev(offset, side)))
    targets.sort(key=lambda target: -target[0])
    for _, target in targets:
        pl.semaphore_signal(barrier, inc=1, device_id=target, device_id_type=MESH)
    greeted = len(targets)

    def relay_send(index):
        for offset in (-relays[index], relays[index]):
            pl.semaphore_signal(relay_sem.at[index], inc=1, device_id=chip_dev(offset, core), device_id_type=MESH)

    def relay_wait(index):
        pl.semaphore_wait(relay_sem.at[index], 2)

    per_tile = 16 // own
    tile = pl.multiple_of(me // per_tile * 16, 16)
    fetches = [
        pltpu.make_async_copy(src, dst, in_sem.at[index])
        for index, (src, dst) in enumerate(
            (
                (proj_hbm, proj),
                (scale_hbm, scale),
                (cot_hbm, cot),
                (reach_hbm, reach_row),
                (skip_hbm, skip_row),
                (filt.at[pl.ds(tile, 16), :], taps_bf),
            )
        )
    ]
    for fetch in fetches:
        fetch.start()
    for fetch in fetches[:-1]:
        fetch.wait()

    wide_rows[...] = jnp.zeros_like(wide_rows)
    for group in range(3):
        wide_rows[2 * group : 2 * group + 2, 0:chans] = jnp.exp2(scale[group].astype(jnp.float32))
    wide_rows[6:7, 0:chans] = skip_row[...]
    reach_len = jnp.zeros((1, chans), jnp.float32)
    for index, divisor in enumerate(REACH_DIVISORS):
        reach_len = jnp.where(reach_row[...] == index, float(seq // divisor), reach_len)
    wide_rows[7:8, 0:chans] = reach_len
    aux[...] = jnp.transpose(wide_rows[...])[0:chans]

    def column(index):
        return aux[:, index : index + 1]

    def dequant(group, half):
        values = proj[group, :, LANES * half : LANES * (half + 1)].astype(jnp.float32)
        return values * column(2 * group + half)

    def upstream(half):
        return cot[:, LANES * half : LANES * (half + 1)].astype(jnp.float32)

    def mixed_of(half):
        return (dequant(1, half) * dequant(2, half)).astype(jnp.bfloat16).astype(jnp.float32)

    def pulled_of(half):
        return (upstream(half) * dequant(0, half)).astype(jnp.bfloat16).astype(jnp.float32)

    flip = exchange_matrix(LANES)

    def reverse(values):
        return jnp.dot(values, flip, preferred_element_type=jnp.float32)

    def reverse_wide(values):
        top = values.astype(jnp.bfloat16)
        rest = (values - top.astype(jnp.float32)).astype(jnp.bfloat16)
        return reverse(top) + reverse(rest)

    for half in range(2):
        send_m[pl.ds(half, chans, stride=2), :] = reverse(mixed_of(half).astype(jnp.bfloat16))
        send_p[pl.ds(half, chans, stride=2), :] = pulled_of(half)

    mine = pl.ds(pl.multiple_of(rows * me, rows), rows)

    def exchange(which, src, dst, urgent=False):
        def copy(peer):
            return pltpu.make_async_remote_copy(
                src_ref=src.at[pl.ds(pl.multiple_of(rows * peer, rows), rows), :],
                dst_ref=dst.at[mine, :],
                send_sem=ctx_send.at[which, peer],
                recv_sem=ctx_recv.at[which, me],
                device_id={"ctx": peer},
                device_id_type=MESH,
            )

        def arrival(peer):
            return pltpu.make_async_remote_copy(
                src_ref=src.at[mine, :],
                dst_ref=dst.at[pl.ds(pl.multiple_of(rows * peer, rows), rows), :],
                send_sem=ctx_send.at[which, me],
                recv_sem=ctx_recv.at[which, peer],
                device_id={"ctx": peer},
                device_id_type=MESH,
            )

        def start():
            def go(step, carry):
                copy(peer_of(step)).start()
                return carry

            if urgent:
                for peer in far_first:
                    copy(peer).start()
            else:
                lax.fori_loop(1, parts, go, 0)
            dst[mine, :] = src[mine, :]

        def wait_recv():
            def go(step, carry):
                arrival(peer_of(step)).wait_recv()
                return carry

            if urgent:
                for peer in reversed(far_first):
                    arrival(peer).wait_recv()
            else:
                lax.fori_loop(1, parts, go, 0)

        def wait_send():
            def go(step, carry):
                copy(peer_of(step)).wait_send()
                return carry

            lax.fori_loop(1, parts, go, 0)

        return start, wait_recv, wait_send

    m_start, m_recv, m_sent = exchange(0, send_m, recv_m, urgent=True)
    p_start, p_recv, p_sent = exchange(1, send_p, recv_p)
    y_start, y_recv, y_sent = exchange(2, send_y, recv_y, urgent=True)
    g_start, g_recv, g_sent = exchange(3, send_g, recv_g)
    f_start, f_recv, f_sent = exchange(4, send_f, recv_f)

    pl.semaphore_wait(barrier, greeted)
    m_start()
    if relays:
        relay_send(0)

    fetches[-1].wait()
    taps[...] = taps_bf[...].astype(jnp.float32)
    lag = lax.broadcasted_iota(jnp.int32, (1, seq), 1).astype(jnp.float32)
    for j in range(own):
        row = taps[pl.ds(me % per_tile * own + j, 1), :]
        reach = aux[pl.ds(me * own + j, 1), :][:, 7:8]
        fine_shifts(jnp.where(lag < reach, row, 0.0), fine.at[j, :, 0:LANES])

    p_start()
    if relays:
        relay_wait(0)
        relay_send(1)

    m_recv()
    zeros = jnp.zeros((parts, LANES), jnp.float32)
    for slot in range(2):
        pads[slot, 0:parts, :] = zeros
    for j in range(own):
        pads[0, parts : 2 * parts, :] = recv_m[pl.ds(2 * j + 1, parts, stride=rows), :]
        pads[1, parts : 2 * parts, :] = recv_m[pl.ds(2 * j, parts, stride=rows), :]
        for n in range(2 * parts + 1):
            at = parts - n // 2
            block = pads[n % 2, at : at + parts, :].astype(jnp.bfloat16)
            if n < 2 * parts:
                left[j, 0:parts, LANES * n : LANES * (n + 1)] = block
            if n >= 1:
                left[j, parts : 2 * parts, LANES * (n - 1) : LANES * n] = block
    for j in range(own):
        out = jnp.dot(left[j], fine[j, :, 0:LANES], preferred_element_type=jnp.float32)
        send_y[pl.ds(2 * j, parts, stride=rows), :] = out[parts:]
        send_y[pl.ds(2 * j + 1, parts, stride=rows), :] = out[:parts]
    y_start()

    def gradients_of(j):
        blocks = [ahead[rows * c + 2 * j + half : rows * c + 2 * j + half + 1, :] for c in range(parts) for half in range(2)]
        fine_shifts(jnp.concatenate(blocks, axis=1), fine.at[j, :, LANES : 2 * LANES])
        for half in range(2):
            pads[half, 0:parts, :] = recv_p[pl.ds(2 * j + half, parts, stride=rows), :]
            pads[half, parts : 2 * parts, :] = zeros
        for n in range(2 * parts + 1):
            at = n // 2
            block = pads[n % 2, at : at + parts, :].astype(jnp.bfloat16)
            if n < 2 * parts:
                left[j, 0:parts, LANES * n : LANES * (n + 1)] = block
            if n >= 1:
                left[j, parts : 2 * parts, LANES * (n - 1) : LANES * n] = block
        out = jnp.dot(left[j], fine[j], preferred_element_type=jnp.float32)
        for half in range(2):
            part = out[parts * half : parts * (half + 1)]
            turned_g[pl.ds(2 * j + half, parts, stride=rows), :] = part[:, :LANES]
            turned_f[pl.ds(2 * j + half, parts, stride=rows), :] = part[:, LANES:]

    ahead[...] = reverse(recv_m[...].astype(jnp.bfloat16))
    gain = column(6)
    for half in range(2):
        query = dequant(0, half)
        factor[:, LANES * half : LANES * (half + 1)] = query * fscale
        offset_term[:, LANES * half : LANES * (half + 1)] = query * (gain * mixed_of(half))
    p_recv()
    for j in range(own // 2):
        gradients_of(j)

    y_recv()
    for half in range(2):
        block = slice(LANES * half, LANES * (half + 1))
        value = factor[:, block] * recv_y[pl.ds(half, chans, stride=2), :] + offset_term[:, block]
        response[:, block] = value
        lm[0, :, block] = jnp.max(jnp.abs(value), axis=0, keepdims=True)

    def conv_of(half):
        return recv_y[pl.ds(half, chans, stride=2), :] * fscale + gain * mixed_of(half)

    def z_step(index):
        return chips // 2 + (index + 1) // 2 * (1 - 2 * (index % 2))

    def z_push(step):
        return pltpu.make_async_remote_copy(
            src_ref=lm.at[0],
            dst_ref=win.at[zpos],
            send_sem=z_send.at[step],
            recv_sem=z_recv.at[zpos],
            device_id=chip_dev(step, core),
            device_id_type=MESH,
        )

    def z_land(step):
        origin = lax.rem(zpos + step, chips)
        return pltpu.make_async_remote_copy(
            src_ref=lm.at[0],
            dst_ref=win.at[origin],
            send_sem=z_send.at[step],
            recv_sem=z_recv.at[origin],
            device_id=chip_dev(step, core),
            device_id_type=MESH,
        )

    def z_start(index, carry):
        z_push(z_step(index)).start()
        return carry

    def z_arrive(index, carry):
        z_land(z_step(chips - 2 - index)).wait_recv()
        return carry

    def z_sent(index, carry):
        z_push(z_step(index)).wait_send()
        return carry

    if relays:
        relay_wait(1)
    lax.fori_loop(0, chips - 1, z_start, 0)
    win[zpos] = lm[0]
    for j in range(own // 2, own):
        gradients_of(j)
    send_g[...] = reverse_wide(turned_g[...])
    g_start()
    send_f[...] = reverse_wide(turned_f[...])
    f_start()

    for half in range(2):
        gr_ref[0, :, LANES * half : LANES * (half + 1)] = (upstream(half) * conv_of(half)).astype(gr_ref.dtype)
    g_recv()
    for half in range(2):
        grad_mixed = recv_g[pl.ds(half, chans, stride=2), :] * fscale + gain * pulled_of(half)
        gr_ref[1, :, LANES * half : LANES * (half + 1)] = (grad_mixed * dequant(2, half)).astype(gr_ref.dtype)
        gr_ref[2, :, LANES * half : LANES * (half + 1)] = (grad_mixed * dequant(1, half)).astype(gr_ref.dtype)
    f_recv()
    reach = column(7)
    for half in range(2):
        lags = (me * (2 * LANES) + half * LANES + lax.broadcasted_iota(jnp.int32, (1, LANES), 1)).astype(jnp.float32)
        fg_ref[:, LANES * half : LANES * (half + 1)] = jnp.where(
            lags < reach, recv_f[pl.ds(half, chans, stride=2), :] * fscale, 0.0
        )


    lax.fori_loop(0, chips - 1, z_arrive, 0)
    wide[0] = jnp.max(win[...], axis=0)
    swap = pltpu.make_async_remote_copy(
        src_ref=wide.at[0],
        dst_ref=other.at[0],
        send_sem=core_sem.at[0],
        recv_sem=core_sem.at[1],
        device_id=chip_dev(0, 1 - core),
        device_id_type=MESH,
    )
    swap.start()
    swap.wait_recv()
    largest = jnp.maximum(wide[0], other[0])
    tm_ref[...] = largest
    so_ref[...] = (response[...] / (largest + 1e-06)).astype(so_ref.dtype)

    for sent in (m_sent, p_sent, y_sent, g_sent, f_sent):
        sent()
    lax.fori_loop(0, chips - 1, z_sent, 0)
    swap.wait_send()


def write_out(*refs):
    count = len(refs) // 2
    sems = refs[-1]
    copies = [pltpu.make_async_copy(refs[index], refs[count + index], sems.at[index]) for index in range(count)]
    for copy in copies:
        copy.start()
    for copy in copies:
        copy.wait()


def body(proj, scale_exp, filt, reach, skip, cotangent):
    groups, chans, span = proj.shape
    parts = lax.axis_size("ctx")
    chips = lax.axis_size("ch") // CORES
    seq = parts * span
    own = chans // parts
    slab = pltpu.VMEM((2 * chans, LANES), jnp.float32)
    hbm = pl.BlockSpec(memory_space=pltpu.HBM)
    vmem = pl.BlockSpec(memory_space=pltpu.VMEM)
    shapes = (
        jax.ShapeDtypeStruct((chans, span), jnp.bfloat16),
        jax.ShapeDtypeStruct((1, span), jnp.float32),
        jax.ShapeDtypeStruct((groups, chans, span), jnp.bfloat16),
        jax.ShapeDtypeStruct((chans, span), jnp.float32),
    )
    results = pl.pallas_call(
        functools.partial(kernel, parts, chips, chans, seq),
        out_shape=shapes,
        in_specs=[hbm] * 6,
        out_specs=(vmem,) * 4,
        scratch_shapes=[slab] * 10
        + [
            pltpu.VMEM((groups, chans, span), jnp.bfloat16),
            pltpu.VMEM((groups, 2, chans), jnp.int32),
            pltpu.VMEM((chans, span), jnp.bfloat16),
            pltpu.VMEM((1, chans), jnp.int32),
            pltpu.VMEM((1, chans), jnp.float32),
            pltpu.VMEM((8, LANES), jnp.float32),
            pltpu.VMEM((chans, 8), jnp.float32),
            pltpu.VMEM((chans, span), jnp.float32),
            pltpu.VMEM((chans, span), jnp.float32),
            pltpu.VMEM((chans, span), jnp.float32),
            pltpu.VMEM((16, seq), jnp.bfloat16),
            pltpu.VMEM((16, seq), jnp.float32),
            pltpu.VMEM((own, seq, 2 * LANES), jnp.bfloat16),
            pltpu.VMEM((2, 2 * parts, LANES), jnp.float32),
            pltpu.VMEM((own, 2 * parts, seq), jnp.bfloat16),
            slab,
            slab,
            slab,
            pltpu.VMEM((1, 1, span), jnp.float32),
            pltpu.VMEM((chips, 1, span), jnp.float32),
            pltpu.VMEM((1, 1, span), jnp.float32),
            pltpu.VMEM((1, 1, span), jnp.float32),
            pltpu.SemaphoreType.DMA((6,)),
            pltpu.SemaphoreType.DMA((5, parts)),
            pltpu.SemaphoreType.DMA((5, parts)),
            pltpu.SemaphoreType.DMA((chips,)),
            pltpu.SemaphoreType.DMA((chips,)),
            pltpu.SemaphoreType.DMA((2,)),
            pltpu.SemaphoreType.REGULAR((2,)),
        ],
        compiler_params=pltpu.CompilerParams(
            collective_id=0, has_side_effects=True, vmem_limit_bytes=40 * 1024 * 1024
        ),
        name="hyena",
    )(
        *(
            pltpu.with_memory_space_constraint(arg, pltpu.HBM)
            for arg in (
                proj,
                jnp.transpose(scale_exp, (0, 2, 1)),
                cotangent,
                filt,
                reach.reshape(1, chans),
                skip.reshape(1, chans),
            )
        )
    )
    scaled_out, token_max, gradients, filter_grad = pl.pallas_call(
        write_out,
        out_shape=shapes,
        in_specs=[pl.BlockSpec(memory_space=pl.ANY)] * 4,
        out_specs=(hbm,) * 4,
        scratch_shapes=[pltpu.SemaphoreType.DMA((4,))],
        compiler_params=pltpu.CompilerParams(vmem_limit_bytes=1024 * 1024),
        name="write_out",
    )(*results)
    return scaled_out, token_max.reshape(span), gradients, filter_grad


def solution(mesh):
    return jax.shard_map(
        body,
        mesh=mesh,
        in_specs=(
            P(None, "ch", "ctx"),
            P(None, "ch", "ctx"),
            P("ch", None),
            P("ch"),
            P("ch"),
            P("ch", "ctx"),
        ),
        out_specs=(P("ch", "ctx"), P("ctx"), P(None, "ch", "ctx"), P("ch", "ctx")),
        check_vma=False,
    )
```

```python
import functools
import math

import jax
import jax.numpy as jnp
from jax import lax
from jax.experimental import pallas as pl
from jax.experimental.pallas import tpu as pltpu
from jax.sharding import PartitionSpec as P

REACH_DIVISORS = (64, 32, 16, 4, 1)
MESH = pl.DeviceIdType.MESH
LANES = 128
CORES = 2


def z_greetings(chips):
    if chips == 32:
        return tuple(range(-4, 5)), (4, 8)
    return tuple(range(chips)), ()


def ctx_hops(offset):
    return sum(min(part, 4 - part) for part in offset)


def ctx_offsets(parts):
    if parts != 16:
        return None
    return sorted(((a, b) for a in range(4) for b in range(4) if a or b), key=lambda offset: -ctx_hops(offset))


def fine_shifts(row, dst):
    width = row.shape[1]
    total = width + LANES
    padded = jnp.concatenate([jnp.zeros((1, LANES), jnp.float32), row], axis=1)
    strip = pltpu.roll(jnp.broadcast_to(padded, (8, total)), 0, 1, stride=1, stride_axis=0)
    strip = jnp.dot(exchange_matrix(8), strip.astype(jnp.bfloat16), preferred_element_type=jnp.float32)
    for k in range(LANES // 16):
        halves = [pltpu.roll(strip, total - by, 1) for by in (16 * k + 8, 16 * k + 16)]
        both = jnp.concatenate(halves, axis=0).astype(jnp.bfloat16)
        for n in range(width // LANES):
            dst[LANES * n + 16 * k : LANES * n + 16 * k + 16, :] = both[:, LANES * n : LANES * (n + 1)]


def exchange_matrix(size):
    total = lax.broadcasted_iota(jnp.int32, (size, size), 0) + lax.broadcasted_iota(jnp.int32, (size, size), 1)
    return (total == size - 1).astype(jnp.float32).astype(jnp.bfloat16)


def kernel(
    parts, chips, chans, seq,
    proj_hbm, scale_hbm, cot_hbm, filt, reach_hbm, skip_hbm,
    so_ref, tm_ref, gr_ref, fg_ref,
    send_m, send_p, send_y, send_g, send_f,
    recv_m, recv_p, recv_y, recv_g, recv_f,
    proj, scale, cot, reach_row, skip_row, wide_rows, aux, response, factor, offset_term,
    taps_bf, taps, fine, pads, left, ahead, turned_g, turned_f,
    lm, win,
    in_sem, ctx_send, ctx_recv, z_send, z_recv, relay_sem,
):
    own = chans // parts
    rows = 2 * own
    fscale = 1.0 / math.sqrt(seq)
    me = lax.axis_index("ctx")
    ch = lax.axis_index("ch")
    zpos = ch // CORES
    core = ch % CORES
    near, relays = z_greetings(chips)

    def peer_of(step):
        return lax.rem(me + step, parts)

    def chip_dev(offset, side):
        return {"ch": lax.rem(zpos + (offset + chips), chips) * CORES + side}

    barrier = pltpu.get_barrier_semaphore()

    offsets = ctx_offsets(parts)
    if offsets is None:
        far_first = [peer_of(step) for step in range(1, parts)]
        targets = [(0, {"ctx": peer}) for peer in far_first]
    else:
        far_first = [lax.rem(me // 4 + a, 4) * 4 + lax.rem(me % 4 + b, 4) for a, b in offsets]
        targets = [(ctx_hops(offset), {"ctx": peer}) for offset, peer in zip(offsets, far_first)]
    for offset in near:
        for side in (1 - core,) if offset == 0 else tuple(range(CORES)):
            targets.append((abs(offset), chip_dev(offset, side)))
    targets.sort(key=lambda target: -target[0])
    for _, target in targets:
        pl.semaphore_signal(barrier, inc=1, device_id=target, device_id_type=MESH)
    greeted = len(targets)

    def relay_send(index):
        for offset in (-relays[index], relays[index]):
            pl.semaphore_signal(relay_sem.at[index], inc=1, device_id=chip_dev(offset, core), device_id_type=MESH)

    def relay_wait(index):
        pl.semaphore_wait(relay_sem.at[index], 2)

    per_tile = 16 // own
    tile = pl.multiple_of(me // per_tile * 16, 16)
    fetches = [
        pltpu.make_async_copy(src, dst, in_sem.at[index])
        for index, (src, dst) in enumerate(
            (
                (proj_hbm, proj),
                (scale_hbm, scale),
                (cot_hbm, cot),
                (reach_hbm, reach_row),
                (skip_hbm, skip_row),
                (filt.at[pl.ds(tile, 16), :], taps_bf),
            )
        )
    ]
    for fetch in fetches:
        fetch.start()
    for fetch in fetches[:-1]:
        fetch.wait()

    wide_rows[...] = jnp.zeros_like(wide_rows)
    for group in range(3):
        wide_rows[2 * group : 2 * group + 2, 0:chans] = jnp.exp2(scale[group].astype(jnp.float32))
    wide_rows[6:7, 0:chans] = skip_row[...]
    reach_len = jnp.zeros((1, chans), jnp.float32)
    for index, divisor in enumerate(REACH_DIVISORS):
        reach_len = jnp.where(reach_row[...] == index, float(seq // divisor), reach_len)
    wide_rows[7:8, 0:chans] = reach_len
    aux[...] = jnp.transpose(wide_rows[...])[0:chans]

    def column(index):
        return aux[:, index : index + 1]

    def dequant(group, half):
        values = proj[group, :, LANES * half : LANES * (half + 1)].astype(jnp.float32)
        return values * column(2 * group + half)

    def upstream(half):
        return cot[:, LANES * half : LANES * (half + 1)].astype(jnp.float32)

    def mixed_of(half):
        return (dequant(1, half) * dequant(2, half)).astype(jnp.bfloat16).astype(jnp.float32)

    def pulled_of(half):
        return (upstream(half) * dequant(0, half)).astype(jnp.bfloat16).astype(jnp.float32)

    flip = exchange_matrix(LANES)

    def reverse(values):
        return jnp.dot(values, flip, preferred_element_type=jnp.float32)

    def reverse_wide(values):
        top = values.astype(jnp.bfloat16)
        rest = (values - top.astype(jnp.float32)).astype(jnp.bfloat16)
        return reverse(top) + reverse(rest)

    for half in range(2):
        send_m[pl.ds(half, chans, stride=2), :] = reverse(mixed_of(half).astype(jnp.bfloat16))
        send_p[pl.ds(half, chans, stride=2), :] = pulled_of(half)

    mine = pl.ds(pl.multiple_of(rows * me, rows), rows)

    def exchange(which, src, dst, urgent=False):
        def copy(peer):
            return pltpu.make_async_remote_copy(
                src_ref=src.at[pl.ds(pl.multiple_of(rows * peer, rows), rows), :],
                dst_ref=dst.at[mine, :],
                send_sem=ctx_send.at[which, peer],
                recv_sem=ctx_recv.at[which, me],
                device_id={"ctx": peer},
                device_id_type=MESH,
            )

        def arrival(peer):
            return pltpu.make_async_remote_copy(
                src_ref=src.at[mine, :],
                dst_ref=dst.at[pl.ds(pl.multiple_of(rows * peer, rows), rows), :],
                send_sem=ctx_send.at[which, me],
                recv_sem=ctx_recv.at[which, peer],
                device_id={"ctx": peer},
                device_id_type=MESH,
            )

        def start():
            def go(step, carry):
                copy(peer_of(step)).start()
                return carry

            if urgent:
                for peer in far_first:
                    copy(peer).start()
            else:
                lax.fori_loop(1, parts, go, 0)
            dst[mine, :] = src[mine, :]

        def wait_recv():
            def go(step, carry):
                arrival(peer_of(step)).wait_recv()
                return carry

            if urgent:
                for peer in reversed(far_first):
                    arrival(peer).wait_recv()
            else:
                lax.fori_loop(1, parts, go, 0)

        def wait_send():
            def go(step, carry):
                copy(peer_of(step)).wait_send()
                return carry

            lax.fori_loop(1, parts, go, 0)

        return start, wait_recv, wait_send

    m_start, m_recv, m_sent = exchange(0, send_m, recv_m, urgent=True)
    p_start, p_recv, p_sent = exchange(1, send_p, recv_p)
    y_start, y_recv, y_sent = exchange(2, send_y, recv_y, urgent=True)
    g_start, g_recv, g_sent = exchange(3, send_g, recv_g)
    f_start, f_recv, f_sent = exchange(4, send_f, recv_f)

    pl.semaphore_wait(barrier, greeted)
    if relays:
        relay_send(0)
    m_start()

    fetches[-1].wait()
    taps[...] = taps_bf[...].astype(jnp.float32)
    lag = lax.broadcasted_iota(jnp.int32, (1, seq), 1).astype(jnp.float32)
    for j in range(own):
        row = taps[pl.ds(me % per_tile * own + j, 1), :]
        reach = aux[pl.ds(me * own + j, 1), :][:, 7:8]
        fine_shifts(jnp.where(lag < reach, row, 0.0), fine.at[j, :, 0:LANES])

    p_start()
    if relays:
        relay_wait(0)
        relay_send(1)

    m_recv()
    zeros = jnp.zeros((parts, LANES), jnp.float32)
    for slot in range(2):
        pads[slot, 0:parts, :] = zeros
    for j in range(own):
        pads[0, parts : 2 * parts, :] = recv_m[pl.ds(2 * j + 1, parts, stride=rows), :]
        pads[1, parts : 2 * parts, :] = recv_m[pl.ds(2 * j, parts, stride=rows), :]
        for n in range(2 * parts + 1):
            at = parts - n // 2
            block = pads[n % 2, at : at + parts, :].astype(jnp.bfloat16)
            if n < 2 * parts:
                left[j, 0:parts, LANES * n : LANES * (n + 1)] = block
            if n >= 1:
                left[j, parts : 2 * parts, LANES * (n - 1) : LANES * n] = block
    for j in range(own):
        out = jnp.dot(left[j], fine[j, :, 0:LANES], preferred_element_type=jnp.float32)
        send_y[pl.ds(2 * j, parts, stride=rows), :] = out[parts:]
        send_y[pl.ds(2 * j + 1, parts, stride=rows), :] = out[:parts]
    y_start()

    def gradients_of(j):
        blocks = [ahead[rows * c + 2 * j + half : rows * c + 2 * j + half + 1, :] for c in range(parts) for half in range(2)]
        fine_shifts(jnp.concatenate(blocks, axis=1), fine.at[j, :, LANES : 2 * LANES])
        for half in range(2):
            pads[half, 0:parts, :] = recv_p[pl.ds(2 * j + half, parts, stride=rows), :]
            pads[half, parts : 2 * parts, :] = zeros
        for n in range(2 * parts + 1):
            at = n // 2
            block = pads[n % 2, at : at + parts, :].astype(jnp.bfloat16)
            if n < 2 * parts:
                left[j, 0:parts, LANES * n : LANES * (n + 1)] = block
            if n >= 1:
                left[j, parts : 2 * parts, LANES * (n - 1) : LANES * n] = block
        out = jnp.dot(left[j], fine[j], preferred_element_type=jnp.float32)
        for half in range(2):
            part = out[parts * half : parts * (half + 1)]
            turned_g[pl.ds(2 * j + half, parts, stride=rows), :] = part[:, :LANES]
            turned_f[pl.ds(2 * j + half, parts, stride=rows), :] = part[:, LANES:]

    ahead[...] = reverse(recv_m[...].astype(jnp.bfloat16))
    gain = column(6)
    for half in range(2):
        query = dequant(0, half)
        factor[:, LANES * half : LANES * (half + 1)] = query * fscale
        offset_term[:, LANES * half : LANES * (half + 1)] = query * (gain * mixed_of(half))

    y_recv()
    peaks = []
    for half in range(2):
        block = slice(LANES * half, LANES * (half + 1))
        value = factor[:, block] * recv_y[pl.ds(half, chans, stride=2), :] + offset_term[:, block]
        response[:, block] = value
        peaks.append(jnp.max(jnp.abs(value), axis=0, keepdims=True))
    lm[0] = jnp.concatenate(peaks, axis=0).astype(jnp.bfloat16)

    def conv_of(half):
        return recv_y[pl.ds(half, chans, stride=2), :] * fscale + gain * mixed_of(half)

    def z_step(index):
        return chips // 2 + (index + 1) // 2 * (1 - 2 * (index % 2))

    def z_push(step, side):
        return pltpu.make_async_remote_copy(
            src_ref=lm.at[0],
            dst_ref=win.at[ch],
            send_sem=z_send.at[CORES * step + side],
            recv_sem=z_recv.at[ch],
            device_id=chip_dev(step, side),
            device_id_type=MESH,
        )

    def z_land(step, side):
        origin = lax.rem(zpos + step, chips) * CORES + side
        return pltpu.make_async_remote_copy(
            src_ref=lm.at[0],
            dst_ref=win.at[origin],
            send_sem=z_send.at[CORES * step + side],
            recv_sem=z_recv.at[origin],
            device_id=chip_dev(step, side),
            device_id_type=MESH,
        )

    def z_start(index, carry):
        for side in range(CORES):
            z_push(z_step(index), side).start()
        return carry

    def z_arrive(index, carry):
        for side in range(CORES):
            z_land(z_step(chips - 2 - index), side).wait_recv()
        return carry

    def z_sent(index, carry):
        for side in range(CORES):
            z_push(z_step(index), side).wait_send()
        return carry

    if relays:
        relay_wait(1)
    lax.fori_loop(0, chips - 1, z_start, 0)
    z_push(0, 1 - core).start()
    win[ch] = lm[0]
    p_recv()
    for j in range(own):
        gradients_of(j)
    send_g[...] = reverse_wide(turned_g[...])
    g_start()
    send_f[...] = reverse_wide(turned_f[...])
    f_start()

    for half in range(2):
        gr_ref[0, :, LANES * half : LANES * (half + 1)] = (upstream(half) * conv_of(half)).astype(gr_ref.dtype)
    g_recv()
    for half in range(2):
        grad_mixed = recv_g[pl.ds(half, chans, stride=2), :] * fscale + gain * pulled_of(half)
        gr_ref[1, :, LANES * half : LANES * (half + 1)] = (grad_mixed * dequant(2, half)).astype(gr_ref.dtype)
        gr_ref[2, :, LANES * half : LANES * (half + 1)] = (grad_mixed * dequant(1, half)).astype(gr_ref.dtype)
    f_recv()
    reach = column(7)
    for half in range(2):
        lags = (me * (2 * LANES) + half * LANES + lax.broadcasted_iota(jnp.int32, (1, LANES), 1)).astype(jnp.float32)
        fg_ref[:, LANES * half : LANES * (half + 1)] = jnp.where(
            lags < reach, recv_f[pl.ds(half, chans, stride=2), :] * fscale, 0.0
        )


    z_land(0, 1 - core).wait_recv()
    lax.fori_loop(0, chips - 1, z_arrive, 0)
    pair = jnp.max(win[...].astype(jnp.float32), axis=0)
    largest = jnp.concatenate([pair[0:1], pair[1:2]], axis=1)
    tm_ref[...] = largest
    so_ref[...] = (response[...] / (largest + 1e-06)).astype(so_ref.dtype)

    for sent in (m_sent, p_sent, y_sent, g_sent, f_sent):
        sent()
    lax.fori_loop(0, chips - 1, z_sent, 0)
    z_push(0, 1 - core).wait_send()


def write_out(*refs):
    count = len(refs) // 2
    sems = refs[-1]
    copies = [pltpu.make_async_copy(refs[index], refs[count + index], sems.at[index]) for index in range(count)]
    for copy in copies:
        copy.start()
    for copy in copies:
        copy.wait()


def body(proj, scale_exp, filt, reach, skip, cotangent):
    groups, chans, span = proj.shape
    parts = lax.axis_size("ctx")
    chips = lax.axis_size("ch") // CORES
    seq = parts * span
    own = chans // parts
    slab = pltpu.VMEM((2 * chans, LANES), jnp.float32)
    hbm = pl.BlockSpec(memory_space=pltpu.HBM)
    vmem = pl.BlockSpec(memory_space=pltpu.VMEM)
    shapes = (
        jax.ShapeDtypeStruct((chans, span), jnp.bfloat16),
        jax.ShapeDtypeStruct((1, span), jnp.float32),
        jax.ShapeDtypeStruct((groups, chans, span), jnp.bfloat16),
        jax.ShapeDtypeStruct((chans, span), jnp.float32),
    )
    results = pl.pallas_call(
        functools.partial(kernel, parts, chips, chans, seq),
        out_shape=shapes,
        in_specs=[hbm] * 6,
        out_specs=(vmem,) * 4,
        scratch_shapes=[slab] * 10
        + [
            pltpu.VMEM((groups, chans, span), jnp.bfloat16),
            pltpu.VMEM((groups, 2, chans), jnp.int32),
            pltpu.VMEM((chans, span), jnp.bfloat16),
            pltpu.VMEM((1, chans), jnp.int32),
            pltpu.VMEM((1, chans), jnp.float32),
            pltpu.VMEM((8, LANES), jnp.float32),
            pltpu.VMEM((chans, 8), jnp.float32),
            pltpu.VMEM((chans, span), jnp.float32),
            pltpu.VMEM((chans, span), jnp.float32),
            pltpu.VMEM((chans, span), jnp.float32),
            pltpu.VMEM((16, seq), jnp.bfloat16),
            pltpu.VMEM((16, seq), jnp.float32),
            pltpu.VMEM((own, seq, 2 * LANES), jnp.bfloat16),
            pltpu.VMEM((2, 2 * parts, LANES), jnp.float32),
            pltpu.VMEM((own, 2 * parts, seq), jnp.bfloat16),
            slab,
            slab,
            slab,
            pltpu.VMEM((1, 2, LANES), jnp.bfloat16),
            pltpu.VMEM((CORES * chips, 2, LANES), jnp.bfloat16),
            pltpu.SemaphoreType.DMA((6,)),
            pltpu.SemaphoreType.DMA((5, parts)),
            pltpu.SemaphoreType.DMA((5, parts)),
            pltpu.SemaphoreType.DMA((CORES * chips,)),
            pltpu.SemaphoreType.DMA((CORES * chips,)),
            pltpu.SemaphoreType.REGULAR((2,)),
        ],
        compiler_params=pltpu.CompilerParams(
            collective_id=0, has_side_effects=True, vmem_limit_bytes=40 * 1024 * 1024
        ),
        name="hyena",
    )(
        *(
            pltpu.with_memory_space_constraint(arg, pltpu.HBM)
            for arg in (
                proj,
                jnp.transpose(scale_exp, (0, 2, 1)),
                cotangent,
                filt,
                reach.reshape(1, chans),
                skip.reshape(1, chans),
            )
        )
    )
    scaled_out, token_max, gradients, filter_grad = pl.pallas_call(
        write_out,
        out_shape=shapes,
        in_specs=[pl.BlockSpec(memory_space=pl.ANY)] * 4,
        out_specs=(hbm,) * 4,
        scratch_shapes=[pltpu.SemaphoreType.DMA((4,))],
        compiler_params=pltpu.CompilerParams(vmem_limit_bytes=1024 * 1024),
        name="write_out",
    )(*results)
    return scaled_out, token_max.reshape(span), gradients, filter_grad


def solution(mesh):
    return jax.shard_map(
        body,
        mesh=mesh,
        in_specs=(
            P(None, "ch", "ctx"),
            P(None, "ch", "ctx"),
            P("ch", None),
            P("ch"),
            P("ch"),
            P("ch", "ctx"),
        ),
        out_specs=(P("ch", "ctx"), P("ctx"), P(None, "ch", "ctx"), P("ch", "ctx")),
        check_vma=False,
    )
```

```python
import functools
import math

import jax
import jax.numpy as jnp
from jax import lax
from jax.experimental import pallas as pl
from jax.experimental.pallas import tpu as pltpu
from jax.sharding import PartitionSpec as P

REACH_DIVISORS = (64, 32, 16, 4, 1)
MESH = pl.DeviceIdType.MESH
LANES = 128
CORES = 2


def z_greetings(chips):
    if chips == 32:
        return tuple(range(-4, 5)), (4, 8)
    return tuple(range(chips)), ()


def ctx_hops(offset):
    return sum(min(part, 4 - part) for part in offset)


def ctx_offsets(parts):
    if parts != 16:
        return None
    return sorted(((a, b) for a in range(4) for b in range(4) if a or b), key=lambda offset: -ctx_hops(offset))


def fine_shifts(row, dst):
    width = row.shape[1]
    total = width + LANES
    padded = jnp.concatenate([jnp.zeros((1, LANES), jnp.float32), row], axis=1)
    strip = pltpu.roll(jnp.broadcast_to(padded, (8, total)), 0, 1, stride=1, stride_axis=0)
    strip = jnp.dot(exchange_matrix(8), strip.astype(jnp.bfloat16), preferred_element_type=jnp.float32)
    for k in range(LANES // 16):
        halves = [pltpu.roll(strip, total - by, 1) for by in (16 * k + 8, 16 * k + 16)]
        both = jnp.concatenate(halves, axis=0).astype(jnp.bfloat16)
        for n in range(width // LANES):
            dst[LANES * n + 16 * k : LANES * n + 16 * k + 16, :] = both[:, LANES * n : LANES * (n + 1)]


def exchange_matrix(size):
    total = lax.broadcasted_iota(jnp.int32, (size, size), 0) + lax.broadcasted_iota(jnp.int32, (size, size), 1)
    return (total == size - 1).astype(jnp.float32).astype(jnp.bfloat16)


def kernel(
    parts, chips, chans, seq,
    proj_hbm, scale_hbm, cot_hbm, filt, reach_hbm, skip_hbm,
    so_ref, tm_ref, gr_ref, fg_ref,
    send_m, send_p, send_y, send_g, send_f,
    recv_m, recv_p, recv_y, recv_g, recv_f,
    proj, scale, cot, reach_row, skip_row, wide_rows, aux, response, factor, offset_term,
    taps_bf, taps, fine, pads, left, ahead, turned_g, turned_f,
    lm, win,
    in_sem, ctx_send, ctx_recv, z_send, z_recv, relay_sem,
):
    own = chans // parts
    rows = 2 * own
    fscale = 1.0 / math.sqrt(seq)
    me = lax.axis_index("ctx")
    ch = lax.axis_index("ch")
    zpos = ch // CORES
    core = ch % CORES
    near, relays = z_greetings(chips)

    def peer_of(step):
        return lax.rem(me + step, parts)

    def chip_dev(offset, side):
        return {"ch": lax.rem(zpos + (offset + chips), chips) * CORES + side}

    barrier = pltpu.get_barrier_semaphore()

    offsets = ctx_offsets(parts)
    if offsets is None:
        far_first = [peer_of(step) for step in range(1, parts)]
        targets = [(0, {"ctx": peer}) for peer in far_first]
    else:
        far_first = [lax.rem(me // 4 + a, 4) * 4 + lax.rem(me % 4 + b, 4) for a, b in offsets]
        targets = [(ctx_hops(offset), {"ctx": peer}) for offset, peer in zip(offsets, far_first)]
    for offset in near:
        for side in (1 - core,) if offset == 0 else tuple(range(CORES)):
            targets.append((abs(offset), chip_dev(offset, side)))
    targets.sort(key=lambda target: -target[0])
    for _, target in targets:
        pl.semaphore_signal(barrier, inc=1, device_id=target, device_id_type=MESH)
    greeted = len(targets)

    def relay_send(index):
        for offset in (-relays[index], relays[index]):
            pl.semaphore_signal(relay_sem.at[index], inc=1, device_id=chip_dev(offset, core), device_id_type=MESH)

    def relay_wait(index):
        pl.semaphore_wait(relay_sem.at[index], 2)

    per_tile = 16 // own
    tile = pl.multiple_of(me // per_tile * 16, 16)
    fetches = [
        pltpu.make_async_copy(src, dst, in_sem.at[index])
        for index, (src, dst) in enumerate(
            (
                (proj_hbm, proj),
                (scale_hbm, scale),
                (cot_hbm, cot),
                (reach_hbm, reach_row),
                (skip_hbm, skip_row),
                (filt.at[pl.ds(tile, 16), :], taps_bf),
            )
        )
    ]
    for fetch in fetches:
        fetch.start()
    for fetch in fetches[:-1]:
        fetch.wait()

    wide_rows[...] = jnp.zeros_like(wide_rows)
    for group in range(3):
        wide_rows[2 * group : 2 * group + 2, 0:chans] = jnp.exp2(scale[group].astype(jnp.float32))
    wide_rows[6:7, 0:chans] = skip_row[...]
    reach_len = jnp.zeros((1, chans), jnp.float32)
    for index, divisor in enumerate(REACH_DIVISORS):
        reach_len = jnp.where(reach_row[...] == index, float(seq // divisor), reach_len)
    wide_rows[7:8, 0:chans] = reach_len
    aux[...] = jnp.transpose(wide_rows[...])[0:chans]

    def column(index):
        return aux[:, index : index + 1]

    def dequant(group, half):
        values = proj[group, :, LANES * half : LANES * (half + 1)].astype(jnp.float32)
        return values * column(2 * group + half)

    def upstream(half):
        return cot[:, LANES * half : LANES * (half + 1)].astype(jnp.float32)

    def mixed_of(half):
        return (dequant(1, half) * dequant(2, half)).astype(jnp.bfloat16).astype(jnp.float32)

    def pulled_of(half):
        return (upstream(half) * dequant(0, half)).astype(jnp.bfloat16).astype(jnp.float32)

    flip = exchange_matrix(LANES)

    def reverse(values):
        return jnp.dot(values, flip, preferred_element_type=jnp.float32)

    def reverse_wide(values):
        top = values.astype(jnp.bfloat16)
        rest = (values - top.astype(jnp.float32)).astype(jnp.bfloat16)
        return reverse(top) + reverse(rest)

    for half in range(2):
        send_m[pl.ds(half, chans, stride=2), :] = reverse(mixed_of(half).astype(jnp.bfloat16))
        send_p[pl.ds(half, chans, stride=2), :] = pulled_of(half)

    mine = pl.ds(pl.multiple_of(rows * me, rows), rows)

    def exchange(which, src, dst, urgent=False):
        def copy(peer):
            return pltpu.make_async_remote_copy(
                src_ref=src.at[pl.ds(pl.multiple_of(rows * peer, rows), rows), :],
                dst_ref=dst.at[mine, :],
                send_sem=ctx_send.at[which, peer],
                recv_sem=ctx_recv.at[which, me],
                device_id={"ctx": peer},
                device_id_type=MESH,
            )

        def arrival(peer):
            return pltpu.make_async_remote_copy(
                src_ref=src.at[mine, :],
                dst_ref=dst.at[pl.ds(pl.multiple_of(rows * peer, rows), rows), :],
                send_sem=ctx_send.at[which, me],
                recv_sem=ctx_recv.at[which, peer],
                device_id={"ctx": peer},
                device_id_type=MESH,
            )

        def start():
            def go(step, carry):
                copy(peer_of(step)).start()
                return carry

            if urgent:
                for peer in far_first:
                    copy(peer).start()
            else:
                lax.fori_loop(1, parts, go, 0)
            dst[mine, :] = src[mine, :]

        def wait_recv():
            def go(step, carry):
                arrival(peer_of(step)).wait_recv()
                return carry

            if urgent:
                for peer in reversed(far_first):
                    arrival(peer).wait_recv()
            else:
                lax.fori_loop(1, parts, go, 0)

        def wait_send():
            def go(step, carry):
                copy(peer_of(step)).wait_send()
                return carry

            lax.fori_loop(1, parts, go, 0)

        return start, wait_recv, wait_send

    m_start, m_recv, m_sent = exchange(0, send_m, recv_m, urgent=True)
    p_start, p_recv, p_sent = exchange(1, send_p, recv_p)
    y_start, y_recv, y_sent = exchange(2, send_y, recv_y, urgent=True)
    g_start, g_recv, g_sent = exchange(3, send_g, recv_g)
    f_start, f_recv, f_sent = exchange(4, send_f, recv_f)

    pl.semaphore_wait(barrier, greeted)
    if relays:
        relay_send(0)
    m_start()

    fetches[-1].wait()
    taps[...] = taps_bf[...].astype(jnp.float32)
    lag = lax.broadcasted_iota(jnp.int32, (1, seq), 1).astype(jnp.float32)
    for j in range(own):
        row = taps[pl.ds(me % per_tile * own + j, 1), :]
        reach = aux[pl.ds(me * own + j, 1), :][:, 7:8]
        fine_shifts(jnp.where(lag < reach, row, 0.0), fine.at[j, :, 0:LANES])

    p_start()
    if relays:
        relay_wait(0)
        relay_send(1)

    m_recv()
    zeros = jnp.zeros((parts, LANES), jnp.float32)
    for slot in range(2):
        pads[slot, 0:parts, :] = zeros
    for j in range(own):
        pads[0, parts : 2 * parts, :] = recv_m[pl.ds(2 * j + 1, parts, stride=rows), :]
        pads[1, parts : 2 * parts, :] = recv_m[pl.ds(2 * j, parts, stride=rows), :]
        for n in range(2 * parts + 1):
            at = parts - n // 2
            block = pads[n % 2, at : at + parts, :].astype(jnp.bfloat16)
            if n < 2 * parts:
                left[j, 0:parts, LANES * n : LANES * (n + 1)] = block
            if n >= 1:
                left[j, parts : 2 * parts, LANES * (n - 1) : LANES * n] = block
    for j in range(own):
        out = jnp.dot(left[j], fine[j, :, 0:LANES], preferred_element_type=jnp.float32)
        send_y[pl.ds(2 * j, parts, stride=rows), :] = out[parts:]
        send_y[pl.ds(2 * j + 1, parts, stride=rows), :] = out[:parts]
    y_start()

    def gradients_of(j):
        blocks = [ahead[rows * c + 2 * j + half : rows * c + 2 * j + half + 1, :] for c in range(parts) for half in range(2)]
        fine_shifts(jnp.concatenate(blocks, axis=1), fine.at[j, :, LANES : 2 * LANES])
        for half in range(2):
            pads[half, 0:parts, :] = recv_p[pl.ds(2 * j + half, parts, stride=rows), :]
            pads[half, parts : 2 * parts, :] = zeros
        for n in range(2 * parts + 1):
            at = n // 2
            block = pads[n % 2, at : at + parts, :].astype(jnp.bfloat16)
            if n < 2 * parts:
                left[j, 0:parts, LANES * n : LANES * (n + 1)] = block
            if n >= 1:
                left[j, parts : 2 * parts, LANES * (n - 1) : LANES * n] = block
        out = jnp.dot(left[j], fine[j], preferred_element_type=jnp.float32)
        for half in range(2):
            part = out[parts * half : parts * (half + 1)]
            turned_g[pl.ds(2 * j + half, parts, stride=rows), :] = part[:, :LANES]
            turned_f[pl.ds(2 * j + half, parts, stride=rows), :] = part[:, LANES:]

    ahead[...] = reverse(recv_m[...].astype(jnp.bfloat16))
    gain = column(6)
    for half in range(2):
        query = dequant(0, half)
        factor[:, LANES * half : LANES * (half + 1)] = query * fscale
        offset_term[:, LANES * half : LANES * (half + 1)] = query * (gain * mixed_of(half))

    y_recv()
    peaks = []
    for half in range(2):
        block = slice(LANES * half, LANES * (half + 1))
        value = factor[:, block] * recv_y[pl.ds(half, chans, stride=2), :] + offset_term[:, block]
        response[:, block] = value
        peaks.append(jnp.max(jnp.abs(value), axis=0, keepdims=True))
    lm[0] = jnp.concatenate(peaks, axis=0).astype(jnp.bfloat16)

    def conv_of(half):
        return recv_y[pl.ds(half, chans, stride=2), :] * fscale + gain * mixed_of(half)

    def z_step(index):
        return chips // 2 + (index + 1) // 2 * (1 - 2 * (index % 2))

    def z_push(step, side):
        return pltpu.make_async_remote_copy(
            src_ref=lm.at[0],
            dst_ref=win.at[ch],
            send_sem=z_send.at[CORES * step + side],
            recv_sem=z_recv.at[ch],
            device_id=chip_dev(step, side),
            device_id_type=MESH,
        )

    def z_land(step, side):
        origin = lax.rem(zpos + step, chips) * CORES + side
        return pltpu.make_async_remote_copy(
            src_ref=lm.at[0],
            dst_ref=win.at[origin],
            send_sem=z_send.at[CORES * step + side],
            recv_sem=z_recv.at[origin],
            device_id=chip_dev(step, side),
            device_id_type=MESH,
        )

    def z_start(index, carry):
        for side in range(CORES):
            z_push(z_step(index), side).start()
        return carry

    def z_arrive(index, carry):
        for side in range(CORES):
            z_land(z_step(chips - 2 - index), side).wait_recv()
        return carry

    def z_sent(index, carry):
        for side in range(CORES):
            z_push(z_step(index), side).wait_send()
        return carry

    if relays:
        relay_wait(1)
    lax.fori_loop(0, chips - 1, z_start, 0)
    z_push(0, 1 - core).start()
    win[ch] = lm[0]
    p_recv()
    for j in range(own):
        gradients_of(j)
    send_g[...] = reverse_wide(turned_g[...])
    g_start()
    send_f[...] = reverse_wide(turned_f[...])
    f_start()

    for half in range(2):
        gr_ref[0, :, LANES * half : LANES * (half + 1)] = (upstream(half) * conv_of(half)).astype(gr_ref.dtype)
    g_recv()
    for half in range(2):
        grad_mixed = recv_g[pl.ds(half, chans, stride=2), :] * fscale + gain * pulled_of(half)
        gr_ref[1, :, LANES * half : LANES * (half + 1)] = (grad_mixed * dequant(2, half)).astype(gr_ref.dtype)
        gr_ref[2, :, LANES * half : LANES * (half + 1)] = (grad_mixed * dequant(1, half)).astype(gr_ref.dtype)
    f_recv()
    reach = column(7)
    for half in range(2):
        lags = (me * (2 * LANES) + half * LANES + lax.broadcasted_iota(jnp.int32, (1, LANES), 1)).astype(jnp.float32)
        fg_ref[:, LANES * half : LANES * (half + 1)] = jnp.where(
            lags < reach, recv_f[pl.ds(half, chans, stride=2), :] * fscale, 0.0
        )


    for sent in (m_sent, p_sent, y_sent, g_sent, f_sent):
        sent()
    lax.fori_loop(0, chips - 1, z_sent, 0)
    z_push(0, 1 - core).wait_send()

    z_land(0, 1 - core).wait_recv()
    lax.fori_loop(0, chips - 1, z_arrive, 0)
    pair = jnp.max(win[...].astype(jnp.float32), axis=0)
    largest = jnp.concatenate([pair[0:1], pair[1:2]], axis=1)
    tm_ref[...] = largest
    so_ref[...] = (response[...] / (largest + 1e-06)).astype(so_ref.dtype)


def write_out(*refs):
    count = len(refs) // 2
    sems = refs[-1]
    copies = [pltpu.make_async_copy(refs[index], refs[count + index], sems.at[index]) for index in range(count)]
    for copy in copies:
        copy.start()
    for copy in copies:
        copy.wait()


def body(proj, scale_exp, filt, reach, skip, cotangent):
    groups, chans, span = proj.shape
    parts = lax.axis_size("ctx")
    chips = lax.axis_size("ch") // CORES
    seq = parts * span
    own = chans // parts
    slab = pltpu.VMEM((2 * chans, LANES), jnp.float32)
    hbm = pl.BlockSpec(memory_space=pltpu.HBM)
    vmem = pl.BlockSpec(memory_space=pltpu.VMEM)
    shapes = (
        jax.ShapeDtypeStruct((chans, span), jnp.bfloat16),
        jax.ShapeDtypeStruct((1, span), jnp.float32),
        jax.ShapeDtypeStruct((groups, chans, span), jnp.bfloat16),
        jax.ShapeDtypeStruct((chans, span), jnp.float32),
    )
    results = pl.pallas_call(
        functools.partial(kernel, parts, chips, chans, seq),
        out_shape=shapes,
        in_specs=[hbm] * 6,
        out_specs=(vmem,) * 4,
        scratch_shapes=[slab] * 10
        + [
            pltpu.VMEM((groups, chans, span), jnp.bfloat16),
            pltpu.VMEM((groups, 2, chans), jnp.int32),
            pltpu.VMEM((chans, span), jnp.bfloat16),
            pltpu.VMEM((1, chans), jnp.int32),
            pltpu.VMEM((1, chans), jnp.float32),
            pltpu.VMEM((8, LANES), jnp.float32),
            pltpu.VMEM((chans, 8), jnp.float32),
            pltpu.VMEM((chans, span), jnp.float32),
            pltpu.VMEM((chans, span), jnp.float32),
            pltpu.VMEM((chans, span), jnp.float32),
            pltpu.VMEM((16, seq), jnp.bfloat16),
            pltpu.VMEM((16, seq), jnp.float32),
            pltpu.VMEM((own, seq, 2 * LANES), jnp.bfloat16),
            pltpu.VMEM((2, 2 * parts, LANES), jnp.float32),
            pltpu.VMEM((own, 2 * parts, seq), jnp.bfloat16),
            slab,
            slab,
            slab,
            pltpu.VMEM((1, 2, LANES), jnp.bfloat16),
            pltpu.VMEM((CORES * chips, 2, LANES), jnp.bfloat16),
            pltpu.SemaphoreType.DMA((6,)),
            pltpu.SemaphoreType.DMA((5, parts)),
            pltpu.SemaphoreType.DMA((5, parts)),
            pltpu.SemaphoreType.DMA((CORES * chips,)),
            pltpu.SemaphoreType.DMA((CORES * chips,)),
            pltpu.SemaphoreType.REGULAR((2,)),
        ],
        compiler_params=pltpu.CompilerParams(
            collective_id=0, has_side_effects=True, vmem_limit_bytes=40 * 1024 * 1024
        ),
        name="hyena",
    )(
        *(
            pltpu.with_memory_space_constraint(arg, pltpu.HBM)
            for arg in (
                proj,
                jnp.transpose(scale_exp, (0, 2, 1)),
                cotangent,
                filt,
                reach.reshape(1, chans),
                skip.reshape(1, chans),
            )
        )
    )
    scaled_out, token_max, gradients, filter_grad = pl.pallas_call(
        write_out,
        out_shape=shapes,
        in_specs=[pl.BlockSpec(memory_space=pl.ANY)] * 4,
        out_specs=(hbm,) * 4,
        scratch_shapes=[pltpu.SemaphoreType.DMA((4,))],
        compiler_params=pltpu.CompilerParams(vmem_limit_bytes=1024 * 1024),
        name="write_out",
    )(*results)
    return scaled_out, token_max.reshape(span), gradients, filter_grad


def solution(mesh):
    return jax.shard_map(
        body,
        mesh=mesh,
        in_specs=(
            P(None, "ch", "ctx"),
            P(None, "ch", "ctx"),
            P("ch", None),
            P("ch"),
            P("ch"),
            P("ch", "ctx"),
        ),
        out_specs=(P("ch", "ctx"), P("ctx"), P(None, "ch", "ctx"), P("ch", "ctx")),
        check_vma=False,
    )
```
